512 devices in a mesh: row: 128 (over x, z, core), rep: 4 (over y).
Axes of the slice: x: 4, y: 4, z: 16, core: 2. Of those that a mesh axis runs over, the one named last changes fastest.
Arguments:
- features: bfloat16 [131072, 256], P('row'), may hold values from -6 to 6
- block_cols: int32 [1024, 4, 12], P('row', 'rep'), may hold values from 0 to 1023, as said below
- block_vals: bfloat16 [1024, 4, 12, 128, 128], P('row', 'rep'), may hold values from -0.078125 to 0.078125
- weight: bfloat16 [256, 256], replicated, may hold values from -0.375 to 0.375
- cotangent: bfloat16 [131072, 256], P(('row', 'rep')), may hold values from -6 to 6
Outputs:
- output_rows: bfloat16 [131072, 256], P(('row', 'rep'))
- grad_weight: float32 [256, 256], replicated
- grad_features: float32 [131072, 256], P(('row', 'rep'))
The draws below stay inside these ranges and needn't reach their ends.
Inputs may be any that keep to these rules, and one draw needn't show every extreme that they name: For a node block b of row group g = b // 8 and quarter index r, every entry block_cols[b, r, s] equals h * 8 + r * 2 + q with h a row group within 3 of g (and inside the grid) and 0 <= q < 2; entries may repeat.
All inputs are finite; a program needn't handle non-finite values.
Results may differ from the reference program's by a relative error of at most 0.0065.
Values may be sent and summed in bfloat16 or wider, within the bound.
No kernel may reach another device: no remote copies, remote signals or barrier semaphores. Data moves between devices by JAX's collectives and lax.ppermute only.
A program may use at most 64 MiB of HBM per device.

```python
import jax
import jax.numpy as jnp
from jax import lax

HID = 256
BLK = 128
BR = 8
HALF = 3
SLOTS = 12
QUART = 2
ROWBLOCKS = 1024
NODES = 131072
N_ROW = 128
N_REP = 4


def draw_block_cols(key, part):
    groups = jnp.arange(ROWBLOCKS) // BR
    lowest = jnp.maximum(groups - HALF, 0)
    highest = jnp.minimum(groups + HALF, N_ROW - 1)
    first_key, second_key = jax.random.split(key)
    dims = (ROWBLOCKS, N_REP, SLOTS)
    source = jax.random.randint(first_key, dims, lowest[:, None, None], highest[:, None, None] + 1)
    within = jax.random.randint(second_key, dims, 0, QUART)
    replica_base = jnp.arange(N_REP)[None, :, None] * QUART
    return (source * BR + replica_base + within).astype(jnp.int32)


def level_of(stream_key, extent, cuts, smallest, top_value):
    def one(position, shards_of):
        steps = jax.random.uniform(jax.random.fold_in(jax.random.fold_in(stream_key, 6), position), (shards_of,), jnp.float32, smallest / len(cuts), top_value / len(cuts))
        return jnp.repeat(jnp.exp(steps), extent[position] // shards_of).reshape((-1,) + (1,) * (len(extent) - position - 1))

    factor_of = one(*cuts[0])
    for cut in cuts[1:]:
        factor_of = factor_of * one(*cut)
    return factor_of


def scatter_about(stream_key, shape, deviation, reach, cuts=(), held_as=jnp.bfloat16):
    entries = deviation * jax.random.normal(stream_key, shape, jnp.float32)
    if cuts:
        entries = entries * level_of(stream_key, shape, cuts, -0.22, 0.18)
    return jnp.clip(entries, -reach, reach).astype(held_as)


def setup_inputs(seed: int = 0) -> dict:
    seeds = jax.random.split(jax.random.key(seed), 6)
    features = scatter_about(seeds[0], (NODES, HID), 1.0, 6.0, ((0, 128),))
    block_cols = draw_block_cols(jax.random.fold_in(seeds[5], 71), 0)
    block_vals = scatter_about(seeds[2], (ROWBLOCKS, N_REP, SLOTS, BLK, BLK), (N_REP * SLOTS * BLK) ** -0.5, 0.078125, ((0, 128), (1, 4)))
    weight = scatter_about(seeds[3], (HID, HID), HID ** -0.5, 0.375)
    cotangent = scatter_about(seeds[4], (NODES, HID), 1.0, 6.0, ((0, 512),))
    return {"features": features, "block_cols": block_cols, "block_vals": block_vals, "weight": weight, "cotangent": cotangent}


def reference(features, block_cols, block_vals, weight, cotangent):
    feature_blocks = features.reshape(ROWBLOCKS, BLK, HID)
    column_ids = block_cols.reshape(ROWBLOCKS, N_REP * SLOTS)
    block_values = block_vals.reshape(ROWBLOCKS, N_REP * SLOTS, BLK, BLK)

    def row_block(payload):
        columns, values = payload
        picked = feature_blocks[columns].astype(jnp.float32)
        return jnp.einsum("sij,sjh->ih", values.astype(jnp.float32), picked)

    aggregate = lax.map(row_block, (column_ids, block_values)).reshape(NODES, HID).astype(jnp.bfloat16)
    preact = jnp.dot(aggregate, weight, preferred_element_type=jnp.float32)
    output_rows = jax.nn.silu(preact).astype(jnp.bfloat16)
    sigmoid_pre = jax.nn.sigmoid(preact)
    grad_pre = (cotangent.astype(jnp.float32) * sigmoid_pre * (1.0 + preact * (1.0 - sigmoid_pre))).astype(jnp.bfloat16)
    grad_weight = jnp.dot(aggregate.T, grad_pre, preferred_element_type=jnp.float32) * (NODES ** -0.5)
    back_rows = jnp.dot(grad_pre, weight.T, preferred_element_type=jnp.float32).astype(jnp.bfloat16)
    back_blocks = back_rows.reshape(ROWBLOCKS, BLK, HID)

    def accumulate(accumulated, payload):
        columns, values, backward = payload
        contribution = jnp.einsum("sji,jh->sih", values.astype(jnp.float32), backward.astype(jnp.float32))
        return accumulated.at[columns].add(contribution), None

    zero_blocks = jnp.zeros((ROWBLOCKS, BLK, HID), jnp.float32)
    grad_blocks, unused = lax.scan(accumulate, zero_blocks, (column_ids, block_values, back_blocks))
    return output_rows, grad_weight, grad_blocks.reshape(NODES, HID)
```

```python
import jax
import jax.numpy as jnp
from jax import lax
from jax.experimental import pallas as pl
from jax.experimental.pallas import tpu as pltpu
from jax.sharding import Mesh
from jax.sharding import PartitionSpec as P

HALF = 3
SECTIONS = 2 * HALF + 1
CORES = 2
X_CHIPS = 4
ROW = ("x", "z", "core")
PLANE = ("x", "core", "rep")
BF16 = jnp.bfloat16
F32 = jnp.float32
PIECE_OF = ((6, 1, 4, 0, 3, 2, 5), (4, 1, 3, 0, 5, 2, 6))


def params(mib=40):
    return pltpu.CompilerParams(vmem_limit_bytes=mib << 20)


def chip_shift(x, by):
    devices = lax.axis_size(ROW)
    by = by * CORES
    return lax.ppermute(x, ROW, [(i, i + by) for i in range(devices) if 0 <= i + by < devices])


def far_shift(x):
    devices = lax.axis_size(ROW)
    pairs = []
    for i in range(devices):
        to = i + HALF if i % CORES else i - HALF
        if 0 <= to < devices:
            pairs.append((i, to))
    return lax.ppermute(x, ROW, pairs)


def core_swap(x):
    return lax.ppermute(x, "core", [(0, 1), (1, 0)])


def transpose_kernel(slot_ref, vals_ref, out_ref, sum_ref):
    block = pl.program_id(0)
    slots = vals_ref.shape[1]
    sum_ref[...] = jnp.zeros_like(sum_ref)
    for s in range(slots):
        at = slot_ref[block * slots + s]
        sum_ref[at] += vals_ref[0, s].astype(F32)
    side = vals_ref.shape[2]
    for c in range(sum_ref.shape[0]):
        out_ref[c * side : (c + 1) * side, :] = sum_ref[c].astype(BF16).T


def transposed_band(slots, vals, columns):
    blocks, count, side, _ = vals.shape
    return pl.pallas_call(
        transpose_kernel,
        grid_spec=pltpu.PrefetchScalarGridSpec(
            num_scalar_prefetch=1,
            grid=(blocks,),
            in_specs=[pl.BlockSpec((1, count, side, side), lambda b, s: (b, 0, 0, 0))],
            out_specs=pl.BlockSpec((columns * side, side), lambda b, s: (0, b)),
            scratch_shapes=[pltpu.VMEM((columns, side, side), F32)],
        ),
        out_shape=jax.ShapeDtypeStruct((columns * side, blocks * side), BF16),
        compiler_params=params(),
        cost_estimate=pl.CostEstimate(flops=0, transcendentals=0, bytes_accessed=16 << 20),
        name="transposed_band",
    )(slots, vals)


def aggregate_kernel(slot_ref, vals_ref, near_ref, other_ref, far_ref, out_ref, window_ref):
    block = pl.program_id(0)
    slots = vals_ref.shape[1]
    side = vals_ref.shape[2]

    @pl.when(block == 0)
    def _():
        at = 0
        for ref in (near_ref, other_ref, far_ref):
            for k in range(ref.shape[0] // side):
                window_ref[at] = ref[k * side : (k + 1) * side, :]
                at += 1

    left = jnp.concatenate([vals_ref[0, s] for s in range(slots)], axis=1)
    right = jnp.concatenate([window_ref[slot_ref[block * slots + s]] for s in range(slots)], axis=0)
    out_ref[0] = jnp.dot(left, right, preferred_element_type=F32).astype(BF16)


def partial_aggregate(slots, vals, near, other, far, reps):
    blocks, count, side, _ = vals.shape
    hidden = near.shape[1]
    per_rep = blocks // reps
    columns = SECTIONS * per_rep

    def whole(x):
        return pl.BlockSpec(x.shape, lambda b, s: (0, 0))

    return pl.pallas_call(
        aggregate_kernel,
        grid_spec=pltpu.PrefetchScalarGridSpec(
            num_scalar_prefetch=1,
            grid=(blocks,),
            in_specs=[
                pl.BlockSpec((1, count, side, side), lambda b, s: (b, 0, 0, 0)),
                whole(near),
                whole(other),
                whole(far),
            ],
            out_specs=pl.BlockSpec((1, side, hidden), lambda b, s: (b // per_rep, b % per_rep, 0)),
            scratch_shapes=[pltpu.VMEM((columns, side, hidden), BF16)],
        ),
        out_shape=jax.ShapeDtypeStruct((reps, per_rep * side, hidden), BF16),
        compiler_params=params(),
        cost_estimate=pl.CostEstimate(flops=1 << 30, transcendentals=0, bytes_accessed=5 << 20),
        name="partial_aggregate",
    )(slots, vals, near, other, far)


def dense_kernel(parts_ref, weight_ref, cotangent_ref, out_ref, send_ref):
    reps, rows, hidden = parts_ref.shape
    summed = parts_ref[0].astype(F32)
    for q in range(1, reps):
        summed = summed + parts_ref[q].astype(F32)
    aggregate = summed.astype(BF16)
    preact = jnp.dot(aggregate, weight_ref[...], preferred_element_type=F32)
    sigmoid_pre = 1.0 / (1.0 + jnp.exp(-preact))
    out_ref[...] = (preact * sigmoid_pre).astype(BF16)
    grad_pre = (
        cotangent_ref[...].astype(F32) * sigmoid_pre * (1.0 + preact * (1.0 - sigmoid_pre))
    ).astype(BF16)
    backward = lax.dot_general(
        grad_pre, weight_ref[...], (((1,), (1,)), ((), ())), preferred_element_type=F32
    ).astype(BF16)
    local = lax.dot_general(
        aggregate, grad_pre, (((0,), (0,)), ((), ())), preferred_element_type=F32
    )
    piece = hidden // (X_CHIPS * CORES * reps)
    for q in range(reps):
        send_ref[q, :rows, :] = backward
        rows_of = [
            local[(k * reps + q) * piece : (k * reps + q + 1) * piece]
            for k in range(X_CHIPS * CORES)
        ]
        send_ref[q, rows:, :] = jnp.concatenate(rows_of, axis=0).astype(BF16)


def dense_layer(parts, weight, cotangent):
    reps, rows, hidden = parts.shape
    return pl.pallas_call(
        dense_kernel,
        out_shape=(
            jax.ShapeDtypeStruct((rows, hidden), BF16),
            jax.ShapeDtypeStruct((reps, rows + hidden // reps, hidden), BF16),
        ),
        compiler_params=params(),
        cost_estimate=pl.CostEstimate(flops=100 << 20, transcendentals=1 << 16, bytes_accessed=2 << 20),
        name="dense_layer",
    )(parts, weight, cotangent)


def products(band_ref, back_ref, first):
    reps = back_ref.shape[0]
    rows = band_ref.shape[1] // reps
    total = None
    for q in range(reps):
        term = jnp.dot(
            band_ref[first : first + rows, q * rows : (q + 1) * rows],
            back_ref[q, :rows, :],
            preferred_element_type=F32,
        )
        total = term if total is None else total + term
    return total


def leaving_kernel(band_ref, back_ref, other_ref, far_ref):
    rows = far_ref.shape[0]
    for k in range(HALF):
        other_ref[k * rows : (k + 1) * rows, :] = products(band_ref, back_ref, (HALF + k) * rows).astype(BF16)
    far_ref[...] = products(band_ref, back_ref, 2 * HALF * rows).astype(BF16)


def staying_kernel(band_ref, back_ref, near_ref):
    rows = near_ref.shape[0] // HALF
    for k in range(HALF):
        near_ref[k * rows : (k + 1) * rows, :] = products(band_ref, back_ref, k * rows)


def window_gradient(band, back, rows):
    hidden = back.shape[2]
    other, far = pl.pallas_call(
        leaving_kernel,
        out_shape=(
            jax.ShapeDtypeStruct((HALF * rows, hidden), BF16),
            jax.ShapeDtypeStruct((rows, hidden), BF16),
        ),
        compiler_params=params(),
        cost_estimate=pl.CostEstimate(flops=1 << 29, transcendentals=0, bytes_accessed=5 << 20),
        name="leaving_gradient",
    )(band, back)
    near = pl.pallas_call(
        staying_kernel,
        out_shape=jax.ShapeDtypeStruct((HALF * rows, hidden), F32),
        compiler_params=params(),
        cost_estimate=pl.CostEstimate(flops=1 << 29, transcendentals=0, bytes_accessed=5 << 20),
        name="staying_gradient",
    )(band, back)
    return near, other, far


def on_device(features, block_cols, block_vals, weight, cotangent):
    reps = lax.axis_size("rep")
    rep = lax.axis_index("rep")
    core = lax.axis_index("core")
    group = lax.axis_index(ROW)
    group_rows, hidden = features.shape
    side = block_vals.shape[-1]
    blocks_group = group_rows // side
    per_rep = blocks_group // reps
    rows = per_rep * side
    columns = SECTIONS * per_rep

    own = lax.dynamic_slice_in_dim(features, rep * rows, rows, 0)
    before = chip_shift(own, 1)
    after = chip_shift(own, -1)
    far = far_shift(own)

    vals = block_vals[:, 0]
    column_ids = block_cols[:, 0, :]
    offset = column_ids // blocks_group - group + HALF
    piece = jnp.zeros_like(column_ids)
    for d in range(SECTIONS):
        piece = jnp.where(offset == d, jnp.where(core == 0, PIECE_OF[0][d], PIECE_OF[1][d]), piece)
    slots = (piece * per_rep + column_ids % blocks_group - rep * per_rep).reshape(-1)
    band = transposed_band(slots, vals, columns)

    near = jnp.concatenate([own, before, after], axis=0)
    other = core_swap(near)
    partial_rows = partial_aggregate(slots, vals, near, other, far, reps)
    parts = lax.all_to_all(partial_rows, "rep", 0, 0, tiled=False)

    output_rows, send = dense_layer(parts, weight, cotangent)
    back = lax.all_to_all(send, "rep", 0, 0, tiled=False)

    plane = X_CHIPS * CORES
    quarter = jnp.sum(back[:, rows:, :].astype(F32), axis=0)
    terms = lax.all_to_all(quarter.reshape(plane, -1, hidden), ("x", "core"), 0, 0, tiled=False)
    line = lax.axis_size("z")
    term = jnp.sum(terms, axis=0).astype(BF16)
    terms = lax.all_to_all(jnp.broadcast_to(term, (line,) + term.shape), "z", 0, 0, tiled=False)
    node_count = group_rows * lax.axis_size(ROW)
    term = jnp.sum(terms.astype(F32), axis=0) * node_count ** (-0.5)
    everyone = plane * reps
    grad_weight = lax.all_to_all(jnp.broadcast_to(term, (everyone,) + term.shape), PLANE, 0, 0, tiled=False)
    grad_weight = grad_weight.reshape(hidden, hidden)

    near_grad, other_grad, far_grad = window_gradient(band, back, rows)
    swapped = core_swap(other_grad)
    from_far = far_shift(far_grad)
    near_grad = near_grad + swapped.astype(F32)
    from_after = chip_shift(near_grad[rows : 2 * rows].astype(BF16), -1)
    from_before = chip_shift(near_grad[2 * rows :].astype(BF16), 1)
    grad_features = (
        near_grad[:rows] + from_after.astype(F32) + from_before.astype(F32) + from_far.astype(F32)
    )
    return output_rows, grad_weight, grad_features


def solution(mesh):
    devices = mesh.devices
    split = Mesh(devices.reshape(X_CHIPS, -1, CORES, devices.shape[1]), ROW + ("rep",))
    everywhere = ROW + ("rep",)
    return jax.shard_map(
        on_device,
        mesh=split,
        in_specs=(
            P(ROW, None),
            P(ROW, "rep", None),
            P(ROW, "rep", None, None, None),
            P(),
            P(everywhere, None),
        ),
        out_specs=(P(everywhere, None), P(), P(everywhere, None)),
        check_vma=False,
    )
```

```python
import jax
import jax.numpy as jnp
from jax import lax
from jax.experimental import pallas as pl
from jax.experimental.pallas import tpu as pltpu
from jax.sharding import Mesh
from jax.sharding import PartitionSpec as P

HALF = 3
SECTIONS = 2 * HALF + 1
CORES = 2
X_CHIPS = 4
ROW = ("x", "z", "core")
PLANE = ("x", "core", "rep")
BF16 = jnp.bfloat16
F32 = jnp.float32
PIECE_OF = ((6, 1, 4, 0, 3, 2, 5), (4, 1, 3, 0, 5, 2, 6))
PIECE_CODE = tuple(sum(p << (4 * d) for d, p in enumerate(row)) for row in PIECE_OF)


def cost(us):
    return pl.CostEstimate(flops=0, transcendentals=0, bytes_accessed=int(us * 3.6e6))


def params(mib):
    return pltpu.CompilerParams(vmem_limit_bytes=mib << 20)


def chip_shift(x, by):
    devices = lax.axis_size(ROW)
    by = by * CORES
    return lax.ppermute(x, ROW, [(i, i + by) for i in range(devices) if 0 <= i + by < devices])


def far_shift(x):
    devices = lax.axis_size(ROW)
    pairs = []
    for i in range(devices):
        to = i + HALF if i % CORES else i - HALF
        if 0 <= to < devices:
            pairs.append((i, to))
    return lax.ppermute(x, ROW, pairs)


def core_swap(x):
    return lax.ppermute(x, "core", [(0, 1), (1, 0)])


def rep_shift(x, by):
    devices = lax.axis_size("rep")
    return lax.ppermute(x, "rep", [(i, (i - by) % devices) for i in range(devices)])


def to_all(x, axes):
    return lax.all_to_all(x, axes, 0, 0, tiled=False)


def band_kernel(blocks_group, per_rep, cols_ref, vals_ref, out_ref, sum_ref):
    block = pl.program_id(0)
    slots, side = vals_ref.shape[1:3]
    group = lax.axis_index(ROW)
    first = lax.axis_index("rep") * per_rep
    code = jnp.where(lax.axis_index("core") == 0, PIECE_CODE[0], PIECE_CODE[1])
    sum_ref[...] = jnp.zeros_like(sum_ref)
    for s in range(slots):
        column = cols_ref[block, 0, s]
        source = lax.div(column, blocks_group)
        piece = lax.shift_right_logical(code, 4 * (source - group + HALF)) & 15
        at = piece * per_rep + column - source * blocks_group - first
        sum_ref[at] += vals_ref[0, s].astype(F32)
    for c in range(sum_ref.shape[0]):
        out_ref[:, c * side : (c + 1) * side] = sum_ref[c].astype(BF16)


def dense_band(cols, vals, blocks_group, per_rep):
    blocks, count, side, _ = vals.shape
    columns = SECTIONS * per_rep

    def kernel(*refs):
        band_kernel(blocks_group, per_rep, *refs)

    return pl.pallas_call(
        kernel,
        grid_spec=pltpu.PrefetchScalarGridSpec(
            num_scalar_prefetch=1,
            grid=(blocks,),
            in_specs=[pl.BlockSpec((1, count, side, side), lambda b, s: (b, 0, 0, 0))],
            out_specs=pl.BlockSpec((side, columns * side), lambda b, s: (b, 0)),
            scratch_shapes=[pltpu.VMEM((columns, side, side), F32)],
        ),
        out_shape=pltpu.HBM((blocks * side, columns * side), BF16),
        compiler_params=params(8),
        cost_estimate=cost(3),
        name="dense_band",
    )(cols, pltpu.with_memory_space_constraint(vals, pltpu.HBM))


def transpose_kernel(band_ref, out_ref):
    out_ref[...] = band_ref[...].T


def transposed(band, side):
    rows, columns = band.shape
    return pl.pallas_call(
        transpose_kernel,
        grid=(rows // side,),
        in_specs=[pl.BlockSpec((side, columns), lambda b: (b, 0))],
        out_specs=pl.BlockSpec((columns, side), lambda b: (0, b)),
        out_shape=pltpu.HBM((columns, rows), BF16),
        compiler_params=params(8),
        cost_estimate=cost(3),
        name="transposed_band",
    )(pltpu.with_memory_space_constraint(band, pltpu.HBM))


def aggregate_kernel(band_ref, near_ref, other_ref, far_ref, out_ref):
    rows, hidden = out_ref.shape[1:]
    total = jnp.zeros((rows, hidden), F32)
    at = 0
    for ref in (near_ref, other_ref, far_ref):
        total = total + jnp.dot(
            band_ref[:, at : at + ref.shape[0]], ref[...], preferred_element_type=F32
        )
        at += ref.shape[0]
    out_ref[0] = total.astype(BF16)


def partial_aggregate(band, near, other, far, reps):
    rows, hidden = band.shape[0] // reps, near.shape[1]

    def whole(x):
        return pl.BlockSpec(x.shape, lambda q: (0, 0))

    return pl.pallas_call(
        aggregate_kernel,
        grid=(reps,),
        in_specs=[pl.BlockSpec((rows, band.shape[1]), lambda q: (q, 0)), whole(near), whole(other), whole(far)],
        out_specs=pl.BlockSpec((1, rows, hidden), lambda q: (q, 0, 0)),
        out_shape=jax.ShapeDtypeStruct((reps, rows, hidden), BF16),
        compiler_params=params(12),
        cost_estimate=cost(1.5),
        name="partial_aggregate",
    )(pltpu.with_memory_space_constraint(band, pltpu.HBM), near, other, far)


def dense_kernel(parts_ref, weight_ref, cotangent_ref, out_ref, back_ref, local_ref):
    reps, rows, hidden = parts_ref.shape
    summed = parts_ref[0].astype(F32)
    for q in range(1, reps):
        summed = summed + parts_ref[q].astype(F32)
    aggregate = summed.astype(BF16)
    preact = jnp.dot(aggregate, weight_ref[...], preferred_element_type=F32)
    sigmoid_pre = 1.0 / (1.0 + jnp.exp(-preact))
    grad_pre = (
        cotangent_ref[...].astype(F32) * sigmoid_pre * (1.0 + preact * (1.0 - sigmoid_pre))
    ).astype(BF16)
    backward = lax.dot_general(
        grad_pre, weight_ref[...], (((1,), (1,)), ((), ())), preferred_element_type=F32
    ).astype(BF16)
    back_ref[...] = backward
    local_ref[...] = lax.dot_general(
        aggregate, grad_pre, (((0,), (0,)), ((), ())), preferred_element_type=F32
    )
    out_ref[...] = (preact * sigmoid_pre).astype(BF16)


def dense_layer(parts, weight, cotangent):
    reps, rows, hidden = parts.shape
    return pl.pallas_call(
        dense_kernel,
        out_shape=(
            jax.ShapeDtypeStruct((rows, hidden), BF16),
            jax.ShapeDtypeStruct((rows, hidden), BF16),
            jax.ShapeDtypeStruct((hidden, hidden), F32),
        ),
        compiler_params=params(8),
        cost_estimate=cost(1.3),
        name="dense_layer",
    )(parts, weight, cotangent)


def gradient_kernel(reps, band_ref, *refs):
    near_ref, other_ref, far_ref = refs[reps:]
    rows, hidden = far_ref.shape
    piece = pl.program_id(0)
    rep = lax.axis_index("rep")
    total = jnp.zeros((rows, hidden), F32)
    for k in range(reps):
        at = pl.multiple_of(lax.rem(rep + k, reps) * rows, rows)
        total = total + jnp.dot(
            band_ref[:, pl.ds(at, rows)], refs[k][...], preferred_element_type=F32
        )

    @pl.when(piece < HALF)
    def _():
        near_ref[pl.ds(pl.multiple_of(piece * rows, rows), rows), :] = total

    @pl.when(jnp.logical_and(piece >= HALF, piece < 2 * HALF))
    def _():
        at = pl.multiple_of((piece - HALF) * rows, rows)
        other_ref[pl.ds(at, rows), :] = total.astype(BF16)

    @pl.when(piece == 2 * HALF)
    def _():
        far_ref[...] = total.astype(BF16)


def window_gradient(band, back):
    reps = len(back)
    rows, hidden = back[0].shape

    def kernel(*refs):
        gradient_kernel(reps, *refs)

    return pl.pallas_call(
        kernel,
        grid=(SECTIONS,),
        in_specs=[pl.BlockSpec((rows, reps * rows), lambda p: (p, 0))]
        + [pl.BlockSpec((rows, hidden), lambda p: (0, 0))] * reps,
        out_specs=[
            pl.BlockSpec((HALF * rows, hidden), lambda p: (0, 0)),
            pl.BlockSpec((HALF * rows, hidden), lambda p: (0, 0)),
            pl.BlockSpec((rows, hidden), lambda p: (0, 0)),
        ],
        out_shape=(
            jax.ShapeDtypeStruct((HALF * rows, hidden), F32),
            jax.ShapeDtypeStruct((HALF * rows, hidden), BF16),
            jax.ShapeDtypeStruct((rows, hidden), BF16),
        ),
        compiler_params=params(16),
        cost_estimate=cost(1.5),
        name="window_gradient",
    )(pltpu.with_memory_space_constraint(band, pltpu.HBM), *back)


def chip_sum_kernel(near_ref, swapped_ref, own_ref, before_ref, after_ref):
    rows = own_ref.shape[0]
    for k, ref in enumerate((own_ref, before_ref, after_ref)):
        at = slice(k * rows, (k + 1) * rows)
        ref[...] = (near_ref[at, :] + swapped_ref[at, :].astype(F32)).astype(ref.dtype)


def chip_sum(near, swapped):
    rows, hidden = near.shape[0] // HALF, near.shape[1]
    return pl.pallas_call(
        chip_sum_kernel,
        out_shape=tuple(jax.ShapeDtypeStruct((rows, hidden), t) for t in (F32, BF16, BF16)),
        compiler_params=params(8),
        cost_estimate=cost(0.5),
        name="chip_sum",
    )(near, swapped)


def spread_kernel(scale, terms_ref, out_ref):
    total = terms_ref[0].astype(F32)
    for k in range(1, terms_ref.shape[0]):
        total = total + terms_ref[k].astype(F32)
    if scale is not None:
        total = total * scale
    total = total.astype(out_ref.dtype)
    for k in range(out_ref.shape[0]):
        out_ref[k] = total


def sum_and_spread(terms, copies, dtype, scale=None):
    def kernel(*refs):
        spread_kernel(scale, *refs)

    return pl.pallas_call(
        kernel,
        out_shape=jax.ShapeDtypeStruct((copies,) + terms.shape[1:], dtype),
        compiler_params=params(8),
        cost_estimate=cost(0.4),
        name="sum_and_spread",
    )(terms)


def on_device(features, block_cols, block_vals, weight, cotangent):
    reps = lax.axis_size("rep")
    rep = lax.axis_index("rep")
    group_rows, hidden = features.shape
    side = block_vals.shape[-1]
    blocks_group = group_rows // side
    per_rep = blocks_group // reps
    rows = per_rep * side

    own = lax.dynamic_slice_in_dim(features, rep * rows, rows, 0)
    before = chip_shift(own, 1)
    after = chip_shift(own, -1)
    far = far_shift(own)
    band = dense_band(block_cols, block_vals[:, 0], blocks_group, per_rep)
    before, after, far, band = lax.optimization_barrier((before, after, far, band))

    near = jnp.concatenate([own, before, after], axis=0)
    other = core_swap(near)
    partial_rows = partial_aggregate(band, near, other, far, reps)
    partial_rows, band = lax.optimization_barrier((partial_rows, band))
    parts = to_all(partial_rows, "rep")
    turned = transposed(band, side)
    parts, turned = lax.optimization_barrier((parts, turned))

    output_rows, backward, local = dense_layer(parts, weight, cotangent)
    back = [backward] + [rep_shift(backward, k) for k in range(1, reps)]

    line = lax.axis_size("z")
    plane = lax.axis_size(PLANE)
    node_count = group_rows * lax.axis_size(ROW)
    terms = to_all(local.reshape(plane, -1, hidden), PLANE)

    spread = sum_and_spread(terms, line, BF16)
    terms = to_all(spread, "z")
    turned, _ = lax.optimization_barrier((turned, spread))
    near_grad, other_grad, far_grad = window_gradient(turned, back)
    swapped = core_swap(other_grad)
    from_far = far_shift(far_grad)
    own_grad, before_grad, after_grad = chip_sum(near_grad, swapped)
    terms, _, _ = lax.optimization_barrier((terms, before_grad, after_grad))
    from_after = chip_shift(before_grad, -1)
    from_before = chip_shift(after_grad, 1)
    terms = to_all(sum_and_spread(terms, plane, F32, node_count ** (-0.5)), PLANE)
    grad_weight = terms.reshape(hidden, hidden)
    grad_features = own_grad + from_after.astype(F32) + from_before.astype(F32) + from_far.astype(F32)
    return output_rows, grad_weight, grad_features


def solution(mesh):
    devices = mesh.devices
    split = Mesh(devices.reshape(X_CHIPS, -1, CORES, devices.shape[1]), ROW + ("rep",))
    everywhere = ROW + ("rep",)
    return jax.shard_map(
        on_device,
        mesh=split,
        in_specs=(
            P(ROW, None),
            P(ROW, "rep", None),
            P(ROW, "rep", None, None, None),
            P(),
            P(everywhere, None),
        ),
        out_specs=(P(everywhere, None), P(), P(everywhere, None)),
        check_vma=False,
    )
```

```python
import jax
import jax.numpy as jnp
from jax import lax
from jax.experimental import pallas as pl
from jax.experimental.pallas import tpu as pltpu
from jax.sharding import Mesh
from jax.sharding import PartitionSpec as P

HALF = 3
SECTIONS = 2 * HALF + 1
CORES = 2
X_CHIPS = 4
ROW = ("x", "z", "core")
PLANE = ("x", "core", "rep")
BF16 = jnp.bfloat16
F32 = jnp.float32
PIECE_OF = ((6, 1, 4, 0, 3, 2, 5), (4, 1, 3, 0, 5, 2, 6))
PIECE_CODE = tuple(sum(p << (4 * d) for d, p in enumerate(row)) for row in PIECE_OF)


GRADIENT_US = 2.0
CHIP_SUM_US = 0.5


def cost(us):
    return pl.CostEstimate(flops=0, transcendentals=0, bytes_accessed=int(us * 3.6e6))


def params(mib):
    return pltpu.CompilerParams(vmem_limit_bytes=mib << 20)


def chip_shift(x, by):
    devices = lax.axis_size(ROW)
    by = by * CORES
    return lax.ppermute(x, ROW, [(i, i + by) for i in range(devices) if 0 <= i + by < devices])


def far_shift(x):
    devices = lax.axis_size(ROW)
    pairs = []
    for i in range(devices):
        to = i + HALF if i % CORES else i - HALF
        if 0 <= to < devices:
            pairs.append((i, to))
    return lax.ppermute(x, ROW, pairs)


def core_swap(x):
    return lax.ppermute(x, "core", [(0, 1), (1, 0)])


def rep_shift(x, by):
    devices = lax.axis_size("rep")
    return lax.ppermute(x, "rep", [(i, (i - by) % devices) for i in range(devices)])


def to_all(x, axes):
    return lax.all_to_all(x, axes, 0, 0, tiled=False)


def band_kernel(blocks_group, per_rep, cols_ref, vals_ref, out_ref, kept_ref, held, sums, arrived, left):
    blocks, slots, side = held.shape[:3]
    columns = sums.shape[0]
    group = lax.axis_index(ROW)
    first = lax.axis_index("rep") * per_rep
    code = jnp.where(lax.axis_index("core") == 0, PIECE_CODE[0], PIECE_CODE[1])

    def fetch(block):
        return pltpu.make_async_copy(vals_ref.at[block], held.at[block], arrived.at[block])

    def rows_of(block):
        return pl.ds(pl.multiple_of(block * side, side), side)

    def keep(block):
        at = rows_of(block)
        return pltpu.make_async_copy(out_ref.at[:, at, :], kept_ref.at[:, at, :], left.at[block])

    for block in range(blocks):
        fetch(block).start()

    def step(block, carry):
        fetch(block).wait()
        sums[...] = jnp.zeros_like(sums)
        for s in range(slots):
            column = cols_ref[block, 0, s]
            source = lax.div(column, blocks_group)
            piece = lax.shift_right_logical(code, 4 * (source - group + HALF)) & 15
            at = piece * per_rep + column - source * blocks_group - first
            sums[at] += held[block, s].astype(F32)
        for c in range(columns):
            lanes = slice(c % per_rep * side, (c % per_rep + 1) * side)
            out_ref[c // per_rep, rows_of(block), lanes] = sums[c].astype(BF16)
        keep(block).start()
        return carry

    lax.fori_loop(0, blocks, step, 0)
    for block in range(blocks):
        keep(block).wait()


def dense_band(cols, vals, blocks_group, per_rep):
    blocks, count, side, _ = vals.shape
    columns = SECTIONS * per_rep
    shape = (SECTIONS, blocks * side, per_rep * side)

    def kernel(*refs):
        band_kernel(blocks_group, per_rep, *refs)

    return pl.pallas_call(
        kernel,
        in_specs=[pl.BlockSpec(memory_space=pltpu.SMEM), pl.BlockSpec(memory_space=pltpu.HBM)],
        out_specs=[pl.BlockSpec(memory_space=pltpu.VMEM), pl.BlockSpec(memory_space=pltpu.HBM)],
        out_shape=[jax.ShapeDtypeStruct(shape, BF16), pltpu.HBM(shape, BF16)],
        scratch_shapes=[
            pltpu.VMEM(vals.shape, BF16),
            pltpu.VMEM((columns, side, side), F32),
            pltpu.SemaphoreType.DMA((blocks,)),
            pltpu.SemaphoreType.DMA((blocks,)),
        ],
        compiler_params=params(16),
        cost_estimate=cost(4),
        name="dense_band",
    )(pltpu.with_memory_space_constraint(cols, pltpu.HBM), pltpu.with_memory_space_constraint(vals, pltpu.HBM))


def aggregate_kernel(band_ref, near_ref, other_ref, far_ref, out_ref):
    reps, rows, hidden = out_ref.shape
    for q in range(reps):
        total = jnp.zeros((rows, hidden), F32)
        piece = 0
        for ref in (near_ref, other_ref, far_ref):
            for k in range(ref.shape[0] // rows):
                total = total + jnp.dot(
                    band_ref[piece, q * rows : (q + 1) * rows, :],
                    ref[k * rows : (k + 1) * rows, :],
                    preferred_element_type=F32,
                )
                piece += 1
        out_ref[q] = total.astype(BF16)


def partial_aggregate(band, near, other, far, reps):
    rows, hidden = band.shape[1] // reps, near.shape[1]
    return pl.pallas_call(
        aggregate_kernel,
        out_shape=jax.ShapeDtypeStruct((reps, rows, hidden), BF16),
        compiler_params=params(12),
        cost_estimate=cost(1.5),
        name="partial_aggregate",
    )(band, near, other, far)


def dense_kernel(parts_ref, weight_ref, cotangent_ref, out_ref, back_ref, local_ref):
    reps, rows, hidden = parts_ref.shape
    summed = parts_ref[0].astype(F32)
    for q in range(1, reps):
        summed = summed + parts_ref[q].astype(F32)
    aggregate = summed.astype(BF16)
    preact = jnp.dot(aggregate, weight_ref[...], preferred_element_type=F32)
    sigmoid_pre = 1.0 / (1.0 + jnp.exp(-preact))
    grad_pre = (
        cotangent_ref[...].astype(F32) * sigmoid_pre * (1.0 + preact * (1.0 - sigmoid_pre))
    ).astype(BF16)
    back_ref[...] = lax.dot_general(
        weight_ref[...], grad_pre, (((1,), (1,)), ((), ())), preferred_element_type=F32
    ).astype(BF16)
    local_ref[...] = lax.dot_general(
        aggregate, grad_pre, (((0,), (0,)), ((), ())), preferred_element_type=F32
    )
    out_ref[...] = (preact * sigmoid_pre).astype(BF16)


def dense_layer(parts, weight, cotangent):
    reps, rows, hidden = parts.shape
    return pl.pallas_call(
        dense_kernel,
        out_shape=(
            jax.ShapeDtypeStruct((rows, hidden), BF16),
            jax.ShapeDtypeStruct((hidden, rows), BF16),
            jax.ShapeDtypeStruct((hidden, hidden), F32),
        ),
        compiler_params=params(8),
        cost_estimate=cost(1.3),
        name="dense_layer",
    )(parts, weight, cotangent)


def gradient_kernel(reps, band_ref, *refs):
    near_ref, other_ref, far_ref, held, arrived = refs[reps:]
    hidden, rows = far_ref.shape
    rep = lax.axis_index("rep")

    def fetch(piece):
        return pltpu.make_async_copy(band_ref.at[piece], held.at[piece], arrived.at[piece])

    order = [*range(HALF, 2 * HALF + 1), *range(HALF)]
    for piece in order:
        fetch(piece).start()
    for piece in order:
        fetch(piece).wait()
        total = jnp.zeros((hidden, rows), F32)
        for k in range(reps):
            at = pl.multiple_of(lax.rem(rep + k, reps) * rows, rows)
            total = total + jnp.dot(
                refs[k][...], held[piece, pl.ds(at, rows), :], preferred_element_type=F32
            )
        if piece < HALF:
            near_ref[piece * hidden : (piece + 1) * hidden, :] = total
        elif piece < 2 * HALF:
            other_ref[(piece - HALF) * hidden : (piece - HALF + 1) * hidden, :] = total.astype(BF16)
        else:
            far_ref[...] = total.astype(BF16)


def window_gradient(band, back):
    reps = len(back)
    hidden, rows = back[0].shape

    def kernel(*refs):
        gradient_kernel(reps, *refs)

    return pl.pallas_call(
        kernel,
        in_specs=[pl.BlockSpec(memory_space=pltpu.HBM)] + [pl.BlockSpec(memory_space=pltpu.VMEM)] * reps,
        out_shape=(
            jax.ShapeDtypeStruct((HALF * hidden, rows), F32),
            jax.ShapeDtypeStruct((HALF * hidden, rows), BF16),
            jax.ShapeDtypeStruct((hidden, rows), BF16),
        ),
        scratch_shapes=[pltpu.VMEM(band.shape, BF16), pltpu.SemaphoreType.DMA((SECTIONS,))],
        compiler_params=params(12),
        cost_estimate=cost(GRADIENT_US),
        name="window_gradient",
    )(pltpu.with_memory_space_constraint(band, pltpu.HBM), *back)


def chip_sum_kernel(near_ref, swapped_ref, own_ref, before_ref, after_ref):
    rows = own_ref.shape[0]
    for k, ref in enumerate((own_ref, before_ref, after_ref)):
        at = slice(k * rows, (k + 1) * rows)
        ref[...] = (near_ref[at, :] + swapped_ref[at, :].astype(F32)).astype(ref.dtype)


def chip_sum(near, swapped):
    rows, hidden = near.shape[0] // HALF, near.shape[1]
    return pl.pallas_call(
        chip_sum_kernel,
        out_shape=tuple(jax.ShapeDtypeStruct((rows, hidden), t) for t in (F32, BF16, BF16)),
        compiler_params=params(8),
        cost_estimate=cost(CHIP_SUM_US),
        name="chip_sum",
    )(near, swapped)


def total_kernel(own_ref, after_ref, before_ref, far_ref, out_ref):
    total = own_ref[...]
    for ref in (after_ref, before_ref, far_ref):
        total = total + ref[...].astype(F32)
    out_ref[...] = total.T


def total_gradient(own, after, before, far):
    hidden, rows = own.shape
    return pl.pallas_call(
        total_kernel,
        out_shape=jax.ShapeDtypeStruct((rows, hidden), F32),
        compiler_params=params(8),
        cost_estimate=cost(0.6),
        name="total_gradient",
    )(own, after, before, far)


def spread_kernel(scale, terms_ref, out_ref):
    total = terms_ref[0].astype(F32)
    for k in range(1, terms_ref.shape[0]):
        total = total + terms_ref[k].astype(F32)
    if scale is not None:
        total = total * scale
    total = total.astype(out_ref.dtype)
    for k in range(out_ref.shape[0]):
        out_ref[k] = total


def sum_and_spread(terms, copies, dtype, scale=None):
    def kernel(*refs):
        spread_kernel(scale, *refs)

    return pl.pallas_call(
        kernel,
        out_shape=jax.ShapeDtypeStruct((copies,) + terms.shape[1:], dtype),
        compiler_params=params(8),
        cost_estimate=cost(0.4),
        name="sum_and_spread",
    )(terms)


def on_device(features, block_cols, block_vals, weight, cotangent):
    reps = lax.axis_size("rep")
    rep = lax.axis_index("rep")
    group_rows, hidden = features.shape
    side = block_vals.shape[-1]
    blocks_group = group_rows // side
    per_rep = blocks_group // reps
    rows = per_rep * side

    own = lax.dynamic_slice_in_dim(features, rep * rows, rows, 0)
    before = chip_shift(own, 1)
    after = chip_shift(own, -1)
    far = far_shift(own)
    band, kept = dense_band(block_cols, block_vals[:, 0], blocks_group, per_rep)
    before, after, far, band = lax.optimization_barrier((before, after, far, band))

    near = jnp.concatenate([own, before, after], axis=0)
    other = core_swap(near)
    parts = to_all(partial_aggregate(band, near, other, far, reps), "rep")

    output_rows, backward, local = dense_layer(parts, weight, cotangent)
    line = lax.axis_size("z")
    plane = lax.axis_size(PLANE)
    node_count = group_rows * lax.axis_size(ROW)
    terms = to_all(local.reshape(plane, -1, hidden), PLANE)
    back = [backward] + [rep_shift(backward, k) for k in range(1, reps)]

    spread = sum_and_spread(terms, line, BF16)
    terms = to_all(spread, "z")
    kept, _ = lax.optimization_barrier((kept, spread))
    near_grad, other_grad, far_grad = window_gradient(kept, back)
    swapped = core_swap(other_grad)
    from_far = far_shift(far_grad)
    own_grad, before_grad, after_grad = chip_sum(near_grad, swapped)
    from_after = chip_shift(before_grad, -1)
    from_before = chip_shift(after_grad, 1)
    terms, from_far, from_after, from_before = lax.optimization_barrier((terms, from_far, from_after, from_before))
    terms = to_all(sum_and_spread(terms, plane, BF16, node_count ** (-0.5)), PLANE)
    grad_weight = terms.reshape(hidden, hidden).astype(F32)
    grad_features = total_gradient(own_grad, from_after, from_before, from_far)
    return output_rows, grad_weight, grad_features


def solution(mesh):
    devices = mesh.devices
    split = Mesh(devices.reshape(X_CHIPS, -1, CORES, devices.shape[1]), ROW + ("rep",))
    everywhere = ROW + ("rep",)
    return jax.shard_map(
        on_device,
        mesh=split,
        in_specs=(
            P(ROW, None),
            P(ROW, "rep", None),
            P(ROW, "rep", None, None, None),
            P(),
            P(everywhere, None),
        ),
        out_specs=(P(everywhere, None), P(), P(everywhere, None)),
        check_vma=False,
    )
```

```python
import jax
import jax.numpy as jnp
from jax import lax
from jax.experimental import pallas as pl
from jax.experimental.pallas import tpu as pltpu
from jax.sharding import Mesh
from jax.sharding import PartitionSpec as P

HALF = 3
SECTIONS = 2 * HALF + 1
CORES = 2
X_CHIPS = 4
ROW = ("x", "z", "core")
PLANE = ("x", "core", "rep")
BF16 = jnp.bfloat16
F32 = jnp.float32
PIECE_OF = ((6, 1, 4, 0, 3, 2, 5), (4, 1, 3, 0, 5, 2, 6))
PIECE_CODE = tuple(sum(p << (4 * d) for d, p in enumerate(row)) for row in PIECE_OF)


GRADIENT_US = 2.0
CHIP_SUM_US = 0.5


def cost(us):
    return pl.CostEstimate(flops=0, transcendentals=0, bytes_accessed=int(us * 3.6e6))


def params(mib):
    return pltpu.CompilerParams(vmem_limit_bytes=mib << 20)


def chip_shift(x, by):
    devices = lax.axis_size(ROW)
    by = by * CORES
    return lax.ppermute(x, ROW, [(i, i + by) for i in range(devices) if 0 <= i + by < devices])


def far_shift(x):
    devices = lax.axis_size(ROW)
    pairs = []
    for i in range(devices):
        to = i + HALF if i % CORES else i - HALF
        if 0 <= to < devices:
            pairs.append((i, to))
    return lax.ppermute(x, ROW, pairs)


def core_swap(x):
    return lax.ppermute(x, "core", [(0, 1), (1, 0)])


def rep_shift(x, by):
    devices = lax.axis_size("rep")
    return lax.ppermute(x, "rep", [(i, (i - by) % devices) for i in range(devices)])


def to_all(x, axes):
    return lax.all_to_all(x, axes, 0, 0, tiled=False)


def quarter_kernel(features_ref, out_ref, arrived):
    rows = out_ref.shape[0]
    at = pl.multiple_of(lax.axis_index("rep") * rows, rows)
    fetch = pltpu.make_async_copy(features_ref.at[pl.ds(at, rows), :], out_ref, arrived)
    fetch.start()
    fetch.wait()


def own_quarter(features, rows):
    return pl.pallas_call(
        quarter_kernel,
        in_specs=[pl.BlockSpec(memory_space=pltpu.HBM)],
        out_specs=pl.BlockSpec(memory_space=pltpu.VMEM),
        out_shape=jax.ShapeDtypeStruct((rows, features.shape[1]), features.dtype),
        scratch_shapes=[pltpu.SemaphoreType.DMA(())],
        compiler_params=params(4),
        cost_estimate=cost(0.5),
        name="own_quarter",
    )(pltpu.with_memory_space_constraint(features, pltpu.HBM))


def band_kernel(blocks_group, per_rep, cols_ref, vals_ref, out_ref, kept_ref, held, sums, arrived, left):
    blocks, slots, side = held.shape[:3]
    columns = sums.shape[0]
    group = lax.axis_index(ROW)
    first = lax.axis_index("rep") * per_rep
    code = jnp.where(lax.axis_index("core") == 0, PIECE_CODE[0], PIECE_CODE[1])

    def fetch(block):
        return pltpu.make_async_copy(vals_ref.at[block], held.at[block], arrived.at[block])

    def rows_of(block):
        return pl.ds(pl.multiple_of(block * side, side), side)

    def keep(block):
        at = rows_of(block)
        return pltpu.make_async_copy(out_ref.at[:, at, :], kept_ref.at[:, at, :], left.at[block])

    for block in range(blocks):
        fetch(block).start(priority=block % 2)

    def step(block, carry):
        fetch(block).wait()
        sums[...] = jnp.zeros_like(sums)
        for s in range(slots):
            column = cols_ref[block, 0, s]
            source = lax.div(column, blocks_group)
            piece = lax.shift_right_logical(code, 4 * (source - group + HALF)) & 15
            at = piece * per_rep + column - source * blocks_group - first
            sums[at] += held[block, s].astype(F32)
        for c in range(columns):
            lanes = slice(c % per_rep * side, (c % per_rep + 1) * side)
            out_ref[c // per_rep, rows_of(block), lanes] = sums[c].astype(BF16)
        keep(block).start()
        return carry

    lax.fori_loop(0, blocks, step, 0)
    for block in range(blocks):
        keep(block).wait()


def dense_band(cols, vals, blocks_group, per_rep):
    blocks, count, side, _ = vals.shape
    columns = SECTIONS * per_rep
    shape = (SECTIONS, blocks * side, per_rep * side)

    def kernel(*refs):
        band_kernel(blocks_group, per_rep, *refs)

    return pl.pallas_call(
        kernel,
        in_specs=[pl.BlockSpec(memory_space=pltpu.SMEM), pl.BlockSpec(memory_space=pltpu.HBM)],
        out_specs=[pl.BlockSpec(memory_space=pltpu.VMEM), pl.BlockSpec(memory_space=pltpu.HBM)],
        out_shape=[jax.ShapeDtypeStruct(shape, BF16), pltpu.HBM(shape, BF16)],
        scratch_shapes=[
            pltpu.VMEM(vals.shape, BF16),
            pltpu.VMEM((columns, side, side), F32),
            pltpu.SemaphoreType.DMA((blocks,)),
            pltpu.SemaphoreType.DMA((blocks,)),
        ],
        compiler_params=params(16),
        cost_estimate=cost(4),
        name="dense_band",
    )(pltpu.with_memory_space_constraint(cols, pltpu.HBM), pltpu.with_memory_space_constraint(vals, pltpu.HBM))


def aggregate_kernel(band_ref, near_ref, other_ref, far_ref, out_ref):
    reps, rows, hidden = out_ref.shape
    for q in range(reps):
        total = jnp.zeros((rows, hidden), F32)
        piece = 0
        for ref in (near_ref, other_ref, far_ref):
            for k in range(ref.shape[0] // rows):
                total = total + jnp.dot(
                    band_ref[piece, q * rows : (q + 1) * rows, :],
                    ref[k * rows : (k + 1) * rows, :],
                    preferred_element_type=F32,
                )
                piece += 1
        out_ref[q] = total.astype(BF16)


def partial_aggregate(band, near, other, far, reps):
    rows, hidden = band.shape[1] // reps, near.shape[1]
    return pl.pallas_call(
        aggregate_kernel,
        out_shape=jax.ShapeDtypeStruct((reps, rows, hidden), BF16),
        compiler_params=params(12),
        cost_estimate=cost(1.5),
        name="partial_aggregate",
    )(band, near, other, far)


def dense_kernel(parts_ref, weight_ref, cotangent_ref, out_ref, back_ref, local_ref):
    reps, rows, hidden = parts_ref.shape
    summed = parts_ref[0].astype(F32)
    for q in range(1, reps):
        summed = summed + parts_ref[q].astype(F32)
    aggregate = summed.astype(BF16)
    preact = jnp.dot(aggregate, weight_ref[...], preferred_element_type=F32)
    sigmoid_pre = 1.0 / (1.0 + jnp.exp(-preact))
    grad_pre = (
        cotangent_ref[...].astype(F32) * sigmoid_pre * (1.0 + preact * (1.0 - sigmoid_pre))
    ).astype(BF16)
    back_ref[...] = lax.dot_general(
        weight_ref[...], grad_pre, (((1,), (1,)), ((), ())), preferred_element_type=F32
    ).astype(BF16)
    local_ref[...] = lax.dot_general(
        aggregate, grad_pre, (((0,), (0,)), ((), ())), preferred_element_type=F32
    )
    out_ref[...] = (preact * sigmoid_pre).astype(BF16)


def dense_layer(parts, weight, cotangent):
    reps, rows, hidden = parts.shape
    return pl.pallas_call(
        dense_kernel,
        out_shape=(
            jax.ShapeDtypeStruct((rows, hidden), BF16),
            jax.ShapeDtypeStruct((hidden, rows), BF16),
            jax.ShapeDtypeStruct((hidden, hidden), F32),
        ),
        compiler_params=params(8),
        cost_estimate=cost(1.3),
        name="dense_layer",
    )(parts, weight, cotangent)


def gradient_kernel(reps, band_ref, *refs):
    near_ref, other_ref, far_ref, held, arrived = refs[reps:]
    hidden, rows = far_ref.shape
    rep = lax.axis_index("rep")

    def fetch(piece):
        return pltpu.make_async_copy(band_ref.at[piece], held.at[piece], arrived.at[piece])

    order = [*range(HALF, 2 * HALF + 1), *range(HALF)]
    for turn, piece in enumerate(order):
        fetch(piece).start(priority=turn % 2)
    for piece in order:
        fetch(piece).wait()
        total = jnp.zeros((hidden, rows), F32)
        for k in range(reps):
            at = pl.multiple_of(lax.rem(rep + k, reps) * rows, rows)
            total = total + jnp.dot(
                refs[k][...], held[piece, pl.ds(at, rows), :], preferred_element_type=F32
            )
        if piece < HALF:
            near_ref[piece * hidden : (piece + 1) * hidden, :] = total
        elif piece < 2 * HALF:
            other_ref[(piece - HALF) * hidden : (piece - HALF + 1) * hidden, :] = total.astype(BF16)
        else:
            far_ref[...] = total.astype(BF16)


def window_gradient(band, back):
    reps = len(back)
    hidden, rows = back[0].shape

    def kernel(*refs):
        gradient_kernel(reps, *refs)

    return pl.pallas_call(
        kernel,
        in_specs=[pl.BlockSpec(memory_space=pltpu.HBM)] + [pl.BlockSpec(memory_space=pltpu.VMEM)] * reps,
        out_shape=(
            jax.ShapeDtypeStruct((HALF * hidden, rows), F32),
            jax.ShapeDtypeStruct((HALF * hidden, rows), BF16),
            jax.ShapeDtypeStruct((hidden, rows), BF16),
        ),
        scratch_shapes=[pltpu.VMEM(band.shape, BF16), pltpu.SemaphoreType.DMA((SECTIONS,))],
        compiler_params=params(12),
        cost_estimate=cost(GRADIENT_US),
        name="window_gradient",
    )(pltpu.with_memory_space_constraint(band, pltpu.HBM), *back)


def chip_sum_kernel(near_ref, swapped_ref, own_ref, before_ref, after_ref):
    rows = own_ref.shape[0]
    for k, ref in enumerate((own_ref, before_ref, after_ref)):
        at = slice(k * rows, (k + 1) * rows)
        ref[...] = (near_ref[at, :] + swapped_ref[at, :].astype(F32)).astype(ref.dtype)


def chip_sum(near, swapped):
    rows, hidden = near.shape[0] // HALF, near.shape[1]
    return pl.pallas_call(
        chip_sum_kernel,
        out_shape=tuple(jax.ShapeDtypeStruct((rows, hidden), t) for t in (F32, BF16, BF16)),
        compiler_params=params(8),
        cost_estimate=cost(CHIP_SUM_US),
        name="chip_sum",
    )(near, swapped)


def total_kernel(own_ref, after_ref, before_ref, far_ref, out_ref):
    total = own_ref[...]
    for ref in (after_ref, before_ref, far_ref):
        total = total + ref[...].astype(F32)
    out_ref[...] = total.T


def total_gradient(own, after, before, far):
    hidden, rows = own.shape
    return pl.pallas_call(
        total_kernel,
        out_shape=jax.ShapeDtypeStruct((rows, hidden), F32),
        compiler_params=params(8),
        cost_estimate=cost(0.6),
        name="total_gradient",
    )(own, after, before, far)


def spread_kernel(scale, terms_ref, out_ref):
    total = terms_ref[0].astype(F32)
    for k in range(1, terms_ref.shape[0]):
        total = total + terms_ref[k].astype(F32)
    if scale is not None:
        total = total * scale
    total = total.astype(out_ref.dtype)
    for k in range(out_ref.shape[0]):
        out_ref[k] = total


def sum_and_spread(terms, copies, dtype, scale=None):
    def kernel(*refs):
        spread_kernel(scale, *refs)

    return pl.pallas_call(
        kernel,
        out_shape=jax.ShapeDtypeStruct((copies,) + terms.shape[1:], dtype),
        compiler_params=params(8),
        cost_estimate=cost(0.4),
        name="sum_and_spread",
    )(terms)


def on_device(features, block_cols, block_vals, weight, cotangent):
    reps = lax.axis_size("rep")
    group_rows, hidden = features.shape
    side = block_vals.shape[-1]
    blocks_group = group_rows // side
    per_rep = blocks_group // reps
    rows = per_rep * side

    own = own_quarter(features, rows)
    before = chip_shift(own, 1)
    after = chip_shift(own, -1)
    far = far_shift(own)
    band, kept = dense_band(block_cols, block_vals[:, 0], blocks_group, per_rep)
    before, after, far, band = lax.optimization_barrier((before, after, far, band))

    near = jnp.concatenate([own, before, after], axis=0)
    other = core_swap(near)
    parts = to_all(partial_aggregate(band, near, other, far, reps), "rep")

    output_rows, backward, local = dense_layer(parts, weight, cotangent)
    line = lax.axis_size("z")
    plane = lax.axis_size(PLANE)
    node_count = group_rows * lax.axis_size(ROW)
    back = [backward] + [rep_shift(backward, k) for k in range(1, reps)]
    local, back[1] = lax.optimization_barrier((local, back[1]))
    terms = to_all(local.reshape(plane, -1, hidden), PLANE)

    spread = sum_and_spread(terms, line, BF16)
    terms = to_all(spread, "z")
    near_grad, other_grad, far_grad = window_gradient(kept, back)
    swapped = core_swap(other_grad)
    from_far = far_shift(far_grad)
    own_grad, before_grad, after_grad = chip_sum(near_grad, swapped)
    from_after = chip_shift(before_grad, -1)
    from_before = chip_shift(after_grad, 1)
    terms, from_far, _, _ = lax.optimization_barrier((terms, from_far, before_grad, after_grad))
    terms = to_all(sum_and_spread(terms, plane, BF16, node_count ** (-0.5)), PLANE)
    grad_weight = terms.reshape(hidden, hidden).astype(F32)
    grad_features = total_gradient(own_grad, from_after, from_before, from_far)
    return output_rows, grad_weight, grad_features


def solution(mesh):
    devices = mesh.devices
    split = Mesh(devices.reshape(X_CHIPS, -1, CORES, devices.shape[1]), ROW + ("rep",))
    everywhere = ROW + ("rep",)
    return jax.shard_map(
        on_device,
        mesh=split,
        in_specs=(
            P(ROW, None),
            P(ROW, "rep", None),
            P(ROW, "rep", None, None, None),
            P(),
            P(everywhere, None),
        ),
        out_specs=(P(everywhere, None), P(), P(everywhere, None)),
        check_vma=False,
    )
```

```python
import jax
import jax.numpy as jnp
from jax import lax
from jax.experimental import pallas as pl
from jax.experimental.pallas import tpu as pltpu
from jax.sharding import Mesh
from jax.sharding import PartitionSpec as P

HALF = 3
SECTIONS = 2 * HALF + 1
CORES = 2
X_CHIPS = 4
ROW = ("x", "z", "core")
PLANE = ("x", "core", "rep")
BF16 = jnp.bfloat16
F32 = jnp.float32
PIECE_OF = ((6, 1, 4, 0, 3, 2, 5), (4, 1, 3, 0, 5, 2, 6))
PIECE_CODE = tuple(sum(p << (4 * d) for d, p in enumerate(row)) for row in PIECE_OF)


GRADIENT_US = 2.0
CHIP_SUM_US = 0.5


def cost(us):
    return pl.CostEstimate(flops=0, transcendentals=0, bytes_accessed=int(us * 3.6e6))


def params(mib):
    return pltpu.CompilerParams(vmem_limit_bytes=mib << 20)


def chip_shift(x, by):
    devices = lax.axis_size(ROW)
    by = by * CORES
    return lax.ppermute(x, ROW, [(i, i + by) for i in range(devices) if 0 <= i + by < devices])


def far_shift(x):
    devices = lax.axis_size(ROW)
    pairs = []
    for i in range(devices):
        to = i + HALF if i % CORES else i - HALF
        if 0 <= to < devices:
            pairs.append((i, to))
    return lax.ppermute(x, ROW, pairs)


def core_swap(x):
    return lax.ppermute(x, "core", [(0, 1), (1, 0)])


def rep_shift(x, by):
    devices = lax.axis_size("rep")
    return lax.ppermute(x, "rep", [(i, (i - by) % devices) for i in range(devices)])


def to_all(x, axes):
    return lax.all_to_all(x, axes, 0, 0, tiled=False)


def quarter_kernel(features_ref, out_ref, arrived):
    rows = out_ref.shape[0]
    at = pl.multiple_of(lax.axis_index("rep") * rows, rows)
    fetch = pltpu.make_async_copy(features_ref.at[pl.ds(at, rows), :], out_ref, arrived)
    fetch.start()
    fetch.wait()


def own_quarter(features, rows):
    return pl.pallas_call(
        quarter_kernel,
        in_specs=[pl.BlockSpec(memory_space=pltpu.HBM)],
        out_specs=pl.BlockSpec(memory_space=pltpu.VMEM),
        out_shape=jax.ShapeDtypeStruct((rows, features.shape[1]), features.dtype),
        scratch_shapes=[pltpu.SemaphoreType.DMA(())],
        compiler_params=params(4),
        cost_estimate=cost(0.5),
        name="own_quarter",
    )(pltpu.with_memory_space_constraint(features, pltpu.HBM))


def band_kernel(blocks_group, per_rep, start, cols_ref, vals_ref, *refs):
    out_ref, held, sums, arrived = refs[-4:]
    blocks, slots, side = held.shape[:3]
    columns = sums.shape[0]
    group = lax.axis_index(ROW)
    first = lax.axis_index("rep") * per_rep
    code = jnp.where(lax.axis_index("core") == 0, PIECE_CODE[0], PIECE_CODE[1])

    def fetch(block):
        return pltpu.make_async_copy(vals_ref.at[start + block], held.at[block], arrived.at[block])

    def rows_of(block):
        return pl.ds(pl.multiple_of((start + block) * side, side), side)

    for block in range(blocks):
        fetch(block).start()

    def step(block, carry):
        fetch(block).wait()
        sums[...] = jnp.zeros_like(sums)
        for s in range(slots):
            column = cols_ref[start + block, 0, s]
            source = lax.div(column, blocks_group)
            piece = lax.shift_right_logical(code, 4 * (source - group + HALF)) & 15
            at = piece * per_rep + column - source * blocks_group - first
            sums[at] += held[block, s].astype(F32)
        for c in range(columns):
            lanes = slice(c % per_rep * side, (c % per_rep + 1) * side)
            out_ref[c // per_rep, rows_of(block), lanes] = sums[c].astype(BF16)
        return carry

    lax.fori_loop(0, blocks, step, 0)


def dense_band(cols, vals, blocks_group, per_rep, start, stop, band=None):
    blocks, count, side, _ = vals.shape
    columns = SECTIONS * per_rep
    built = stop - start

    def kernel(*refs):
        band_kernel(blocks_group, per_rep, start, *refs)

    args = [pltpu.with_memory_space_constraint(cols, pltpu.HBM), pltpu.with_memory_space_constraint(vals, pltpu.HBM)]
    specs = [pl.BlockSpec(memory_space=pltpu.SMEM), pl.BlockSpec(memory_space=pltpu.HBM)]
    if band is not None:
        args.append(band)
        specs.append(pl.BlockSpec(memory_space=pltpu.VMEM))
    return pl.pallas_call(
        kernel,
        in_specs=specs,
        out_specs=pl.BlockSpec(memory_space=pltpu.VMEM),
        out_shape=jax.ShapeDtypeStruct((SECTIONS, blocks * side, per_rep * side), BF16),
        input_output_aliases={} if band is None else {2: 0},
        scratch_shapes=[
            pltpu.VMEM((built, count, side, side), BF16),
            pltpu.VMEM((columns, side, side), F32),
            pltpu.SemaphoreType.DMA((built,)),
        ],
        compiler_params=params(16),
        cost_estimate=cost(2),
        name="dense_band",
    )(*args)


def aggregate_kernel(band_ref, near_ref, other_ref, far_ref, out_ref):
    reps, rows, hidden = out_ref.shape
    for q in range(reps):
        total = jnp.zeros((rows, hidden), F32)
        piece = 0
        for ref in (near_ref, other_ref, far_ref):
            for k in range(ref.shape[0] // rows):
                total = total + jnp.dot(
                    band_ref[piece, q * rows : (q + 1) * rows, :],
                    ref[k * rows : (k + 1) * rows, :],
                    preferred_element_type=F32,
                )
                piece += 1
        out_ref[q] = total.astype(BF16)


def partial_aggregate(band, near, other, far, reps):
    rows, hidden = band.shape[1] // reps, near.shape[1]
    return pl.pallas_call(
        aggregate_kernel,
        out_shape=jax.ShapeDtypeStruct((reps, rows, hidden), BF16),
        compiler_params=params(12),
        cost_estimate=cost(1.5),
        name="partial_aggregate",
    )(band, near, other, far)


def dense_kernel(parts_ref, weight_ref, cotangent_ref, out_ref, back_ref, quarter_ref, *refs):
    reps, rows, hidden = parts_ref.shape
    *send_refs, local_ref = refs
    summed = parts_ref[0].astype(F32)
    for q in range(1, reps):
        summed = summed + parts_ref[q].astype(F32)
    aggregate = summed.astype(BF16)
    preact = jnp.dot(aggregate, weight_ref[...], preferred_element_type=F32)
    sigmoid_pre = 1.0 / (1.0 + jnp.exp(-preact))
    grad_pre = (
        cotangent_ref[...].astype(F32) * sigmoid_pre * (1.0 + preact * (1.0 - sigmoid_pre))
    ).astype(BF16)
    backward = lax.dot_general(
        weight_ref[...], grad_pre, (((1,), (1,)), ((), ())), preferred_element_type=F32
    ).astype(BF16)
    back_ref[...] = backward
    local_ref[...] = lax.dot_general(
        aggregate, grad_pre, (((0,), (0,)), ((), ())), preferred_element_type=F32
    )
    plane = X_CHIPS * CORES
    piece = hidden // (plane * reps)
    rep = lax.axis_index("rep")
    for k in range(reps):
        of_rep = []
        for i in range(plane):
            at = pl.multiple_of((i * reps + lax.rem(rep + reps - k, reps)) * piece, piece)
            of_rep.append(local_ref[pl.ds(at, piece), :])
        quarter = jnp.concatenate(of_rep, axis=0)
        if k == 0:
            quarter_ref[...] = quarter
        else:
            send_refs[k - 1][:hidden, :] = backward
            send_refs[k - 1][hidden:, :] = quarter.astype(BF16)
    out_ref[...] = (preact * sigmoid_pre).astype(BF16)


def dense_layer(parts, weight, cotangent):
    reps, rows, hidden = parts.shape
    quarter = hidden // reps
    return pl.pallas_call(
        dense_kernel,
        out_shape=[
            jax.ShapeDtypeStruct((rows, hidden), BF16),
            jax.ShapeDtypeStruct((hidden, rows), BF16),
            jax.ShapeDtypeStruct((quarter, hidden), F32),
        ]
        + [jax.ShapeDtypeStruct((hidden + quarter, rows), BF16)] * (reps - 1),
        scratch_shapes=[pltpu.VMEM((hidden, hidden), F32)],
        compiler_params=params(8),
        cost_estimate=cost(1.3),
        name="dense_layer",
    )(parts, weight, cotangent)


def gradient_kernel(reps, band_ref, quarter_ref, *refs):
    near_ref, other_ref, far_ref, sum_ref = refs[reps:]
    hidden, rows = far_ref.shape
    rep = lax.axis_index("rep")

    def product(piece):
        total = jnp.zeros((hidden, rows), F32)
        for k in range(reps):
            at = pl.multiple_of(lax.rem(rep + k, reps) * rows, rows)
            total = total + jnp.dot(
                refs[k][:hidden, :], band_ref[piece, pl.ds(at, rows), :], preferred_element_type=F32
            )
        return total

    total = quarter_ref[...]
    for k in range(1, reps):
        total = total + refs[k][hidden:, :].astype(F32)
    sum_ref[...] = total
    for k in range(HALF):
        at = slice(k * hidden, (k + 1) * hidden)
        other_ref[at, :] = product(HALF + k).astype(BF16)
        near_ref[at, :] = product(k)
    far_ref[...] = product(2 * HALF).astype(BF16)


def window_gradient(band, quarter, back):
    reps = len(back)
    hidden, rows = back[0].shape

    def kernel(*refs):
        gradient_kernel(reps, *refs)

    return pl.pallas_call(
        kernel,
        out_shape=(
            jax.ShapeDtypeStruct((HALF * hidden, rows), F32),
            jax.ShapeDtypeStruct((HALF * hidden, rows), BF16),
            jax.ShapeDtypeStruct((hidden, rows), BF16),
            jax.ShapeDtypeStruct(quarter.shape, F32),
        ),
        compiler_params=params(12),
        cost_estimate=cost(GRADIENT_US),
        name="window_gradient",
    )(band, quarter, *back)


def chip_sum_kernel(near_ref, swapped_ref, own_ref, before_ref, after_ref):
    rows = own_ref.shape[0]
    for k, ref in enumerate((own_ref, before_ref, after_ref)):
        at = slice(k * rows, (k + 1) * rows)
        ref[...] = (near_ref[at, :] + swapped_ref[at, :].astype(F32)).astype(ref.dtype)


def chip_sum(near, swapped):
    rows, hidden = near.shape[0] // HALF, near.shape[1]
    return pl.pallas_call(
        chip_sum_kernel,
        out_shape=tuple(jax.ShapeDtypeStruct((rows, hidden), t) for t in (F32, BF16, BF16)),
        compiler_params=params(8),
        cost_estimate=cost(CHIP_SUM_US),
        name="chip_sum",
    )(near, swapped)


def total_kernel(own_ref, after_ref, before_ref, far_ref, out_ref):
    total = own_ref[...]
    for ref in (after_ref, before_ref, far_ref):
        total = total + ref[...].astype(F32)
    out_ref[...] = total.T


def total_gradient(own, after, before, far):
    hidden, rows = own.shape
    return pl.pallas_call(
        total_kernel,
        out_shape=jax.ShapeDtypeStruct((rows, hidden), F32),
        compiler_params=params(8),
        cost_estimate=cost(0.6),
        name="total_gradient",
    )(own, after, before, far)


def spread_kernel(scale, terms_ref, out_ref):
    total = terms_ref[0].astype(F32)
    for k in range(1, terms_ref.shape[0]):
        total = total + terms_ref[k].astype(F32)
    if scale is not None:
        total = total * scale
    total = total.astype(out_ref.dtype)
    for k in range(out_ref.shape[0]):
        out_ref[k] = total


def sum_and_spread(terms, copies, dtype, scale=None):
    def kernel(*refs):
        spread_kernel(scale, *refs)

    return pl.pallas_call(
        kernel,
        out_shape=jax.ShapeDtypeStruct((copies,) + terms.shape[1:], dtype),
        compiler_params=params(8),
        cost_estimate=cost(0.4),
        name="sum_and_spread",
    )(terms)


def on_device(features, block_cols, block_vals, weight, cotangent):
    reps = lax.axis_size("rep")
    group_rows, hidden = features.shape
    side = block_vals.shape[-1]
    blocks_group = group_rows // side
    per_rep = blocks_group // reps
    rows = per_rep * side

    own = own_quarter(features, rows)
    before = chip_shift(own, 1)
    after = chip_shift(own, -1)
    far = far_shift(own)
    vals = block_vals[:, 0]
    half = blocks_group // 2
    band = dense_band(block_cols, vals, blocks_group, per_rep, 0, half)
    before, after, far, band = lax.optimization_barrier((before, after, far, band))

    near = jnp.concatenate([own, before, after], axis=0)
    near, band = lax.optimization_barrier((near, band))
    other = core_swap(near)
    band = dense_band(block_cols, vals, blocks_group, per_rep, half, blocks_group, band)
    parts = to_all(partial_aggregate(band, near, other, far, reps), "rep")

    output_rows, backward, quarter, *sends = dense_layer(parts, weight, cotangent)
    back = [backward] + [rep_shift(send, k + 1) for k, send in enumerate(sends)]
    line = lax.axis_size("z")
    plane = lax.axis_size(("x", "core"))
    node_count = group_rows * lax.axis_size(ROW)
    near_grad, other_grad, far_grad, quarter = window_gradient(band, quarter, back)
    terms = to_all(quarter.reshape(plane, -1, hidden), ("x", "core"))
    swapped = core_swap(other_grad)
    from_far = far_shift(far_grad)
    terms = to_all(sum_and_spread(terms, line, BF16), "z")
    own_grad, before_grad, after_grad = chip_sum(near_grad, swapped)
    from_after = chip_shift(before_grad, -1)
    from_before = chip_shift(after_grad, 1)
    terms, from_far, _, _ = lax.optimization_barrier((terms, from_far, before_grad, after_grad))
    terms = to_all(sum_and_spread(terms, plane * reps, BF16, node_count ** (-0.5)), PLANE)
    grad_features = total_gradient(own_grad, from_after, from_before, from_far)
    terms, grad_features = lax.optimization_barrier((terms, grad_features))
    grad_weight = terms.reshape(hidden, hidden).astype(F32)
    return output_rows, grad_weight, grad_features


def solution(mesh):
    devices = mesh.devices
    split = Mesh(devices.reshape(X_CHIPS, -1, CORES, devices.shape[1]), ROW + ("rep",))
    everywhere = ROW + ("rep",)
    return jax.shard_map(
        on_device,
        mesh=split,
        in_specs=(
            P(ROW, None),
            P(ROW, "rep", None),
            P(ROW, "rep", None, None, None),
            P(),
            P(everywhere, None),
        ),
        out_specs=(P(everywhere, None), P(), P(everywhere, None)),
        check_vma=False,
    )
```

```python
import jax
import jax.numpy as jnp
from jax import lax
from jax.experimental import pallas as pl
from jax.experimental.pallas import tpu as pltpu
from jax.sharding import Mesh
from jax.sharding import PartitionSpec as P

HALF = 3
SECTIONS = 2 * HALF + 1
CORES = 2
X_CHIPS = 4
ROW = ("x", "z", "core")
PLANE = ("x", "core", "rep")
BF16 = jnp.bfloat16
F32 = jnp.float32
PIECE_OF = ((6, 1, 4, 0, 3, 2, 5), (4, 1, 3, 0, 5, 2, 6))
PIECE_CODE = tuple(sum(p << (4 * d) for d, p in enumerate(row)) for row in PIECE_OF)


GRADIENT_US = 2.0
CHIP_SUM_US = 0.5


def cost(us):
    return pl.CostEstimate(flops=0, transcendentals=0, bytes_accessed=int(us * 3.6e6))


def params(mib):
    return pltpu.CompilerParams(vmem_limit_bytes=mib << 20)


def chip_shift(x, by):
    devices = lax.axis_size(ROW)
    by = by * CORES
    return lax.ppermute(x, ROW, [(i, i + by) for i in range(devices) if 0 <= i + by < devices])


def far_shift(x):
    devices = lax.axis_size(ROW)
    pairs = []
    for i in range(devices):
        to = i + HALF if i % CORES else i - HALF
        if 0 <= to < devices:
            pairs.append((i, to))
    return lax.ppermute(x, ROW, pairs)


def core_swap(x):
    return lax.ppermute(x, "core", [(0, 1), (1, 0)])


def rep_shift(x, by):
    devices = lax.axis_size("rep")
    return lax.ppermute(x, "rep", [(i, (i - by) % devices) for i in range(devices)])


def to_all(x, axes):
    return lax.all_to_all(x, axes, 0, 0, tiled=False)


def quarter_kernel(features_ref, out_ref, arrived):
    rows = out_ref.shape[0]
    at = pl.multiple_of(lax.axis_index("rep") * rows, rows)
    fetch = pltpu.make_async_copy(features_ref.at[pl.ds(at, rows), :], out_ref, arrived)
    fetch.start()
    fetch.wait()


def own_quarter(features, rows):
    return pl.pallas_call(
        quarter_kernel,
        in_specs=[pl.BlockSpec(memory_space=pltpu.HBM)],
        out_specs=pl.BlockSpec(memory_space=pltpu.VMEM),
        out_shape=jax.ShapeDtypeStruct((rows, features.shape[1]), features.dtype),
        scratch_shapes=[pltpu.SemaphoreType.DMA(())],
        compiler_params=params(4),
        cost_estimate=cost(0.5),
        name="own_quarter",
    )(pltpu.with_memory_space_constraint(features, pltpu.HBM))


def band_kernel(blocks_group, per_rep, cols_ref, vals_ref, out_ref, held, sums, arrived):
    blocks, slots, side = held.shape[:3]
    columns = sums.shape[0]
    group = lax.axis_index(ROW)
    first = lax.axis_index("rep") * per_rep
    code = jnp.where(lax.axis_index("core") == 0, PIECE_CODE[0], PIECE_CODE[1])

    def fetch(block):
        return pltpu.make_async_copy(vals_ref.at[block], held.at[block], arrived.at[block])

    def rows_of(block):
        return pl.ds(pl.multiple_of(block * side, side), side)

    for block in range(blocks):
        fetch(block).start()

    def step(block, carry):
        fetch(block).wait()
        sums[...] = jnp.zeros_like(sums)
        for s in range(slots):
            column = cols_ref[block, 0, s]
            source = lax.div(column, blocks_group)
            piece = lax.shift_right_logical(code, 4 * (source - group + HALF)) & 15
            at = piece * per_rep + column - source * blocks_group - first
            sums[at] += held[block, s].astype(F32)
        for c in range(columns):
            lanes = slice(c % per_rep * side, (c % per_rep + 1) * side)
            out_ref[c // per_rep, rows_of(block), lanes] = sums[c].astype(BF16)
        return carry

    lax.fori_loop(0, blocks, step, 0)


def dense_band(cols, vals, blocks_group, per_rep):
    blocks, count, side, _ = vals.shape
    columns = SECTIONS * per_rep
    shape = (SECTIONS, blocks * side, per_rep * side)

    def kernel(*refs):
        band_kernel(blocks_group, per_rep, *refs)

    return pl.pallas_call(
        kernel,
        in_specs=[pl.BlockSpec(memory_space=pltpu.SMEM), pl.BlockSpec(memory_space=pltpu.HBM)],
        out_specs=pl.BlockSpec(memory_space=pltpu.VMEM),
        out_shape=jax.ShapeDtypeStruct(shape, BF16),
        scratch_shapes=[
            pltpu.VMEM(vals.shape, BF16),
            pltpu.VMEM((columns, side, side), F32),
            pltpu.SemaphoreType.DMA((blocks,)),
        ],
        compiler_params=params(16),
        cost_estimate=cost(4),
        name="dense_band",
    )(pltpu.with_memory_space_constraint(cols, pltpu.HBM), pltpu.with_memory_space_constraint(vals, pltpu.HBM))


def aggregate_kernel(band_ref, near_ref, other_ref, far_ref, out_ref):
    reps, rows, hidden = out_ref.shape
    for q in range(reps):
        total = jnp.zeros((rows, hidden), F32)
        piece = 0
        for ref in (near_ref, other_ref, far_ref):
            for k in range(ref.shape[0] // rows):
                total = total + jnp.dot(
                    band_ref[piece, q * rows : (q + 1) * rows, :],
                    ref[k * rows : (k + 1) * rows, :],
                    preferred_element_type=F32,
                )
                piece += 1
        out_ref[q] = total.astype(BF16)


def partial_aggregate(band, near, other, far, reps):
    rows, hidden = band.shape[1] // reps, near.shape[1]
    return pl.pallas_call(
        aggregate_kernel,
        out_shape=jax.ShapeDtypeStruct((reps, rows, hidden), BF16),
        compiler_params=params(12),
        cost_estimate=cost(1.5),
        name="partial_aggregate",
    )(band, near, other, far)


def dense_kernel(parts_ref, weight_ref, cotangent_ref, out_ref, back_ref, local_ref):
    reps, rows, hidden = parts_ref.shape
    summed = parts_ref[0].astype(F32)
    for q in range(1, reps):
        summed = summed + parts_ref[q].astype(F32)
    aggregate = summed.astype(BF16)
    preact = jnp.dot(aggregate, weight_ref[...], preferred_element_type=F32)
    sigmoid_pre = 1.0 / (1.0 + jnp.exp(-preact))
    grad_pre = (
        cotangent_ref[...].astype(F32) * sigmoid_pre * (1.0 + preact * (1.0 - sigmoid_pre))
    ).astype(BF16)
    back_ref[...] = lax.dot_general(
        weight_ref[...], grad_pre, (((1,), (1,)), ((), ())), preferred_element_type=F32
    ).astype(BF16)
    local_ref[...] = lax.dot_general(
        aggregate, grad_pre, (((0,), (0,)), ((), ())), preferred_element_type=F32
    )
    out_ref[...] = (preact * sigmoid_pre).astype(BF16)


def dense_layer(parts, weight, cotangent):
    reps, rows, hidden = parts.shape
    return pl.pallas_call(
        dense_kernel,
        out_shape=(
            jax.ShapeDtypeStruct((rows, hidden), BF16),
            jax.ShapeDtypeStruct((hidden, rows), BF16),
            jax.ShapeDtypeStruct((hidden, hidden), F32),
        ),
        compiler_params=params(8),
        cost_estimate=cost(1.3),
        name="dense_layer",
    )(parts, weight, cotangent)


def gradient_kernel(reps, band_ref, *refs):
    near_ref, other_ref, far_ref, held, arrived = refs[reps:]
    hidden, rows = far_ref.shape
    rep = lax.axis_index("rep")

    def fetch(piece):
        return pltpu.make_async_copy(band_ref.at[piece], held.at[piece], arrived.at[piece])

    order = [*range(HALF, 2 * HALF + 1), *range(HALF)]
    for piece in order:
        fetch(piece).start()
    for piece in order:
        fetch(piece).wait()
        total = jnp.zeros((hidden, rows), F32)
        for k in range(reps):
            at = pl.multiple_of(lax.rem(rep + k, reps) * rows, rows)
            total = total + jnp.dot(
                refs[k][...], held[piece, pl.ds(at, rows), :], preferred_element_type=F32
            )
        if piece < HALF:
            near_ref[piece * hidden : (piece + 1) * hidden, :] = total
        elif piece < 2 * HALF:
            other_ref[(piece - HALF) * hidden : (piece - HALF + 1) * hidden, :] = total.astype(BF16)
        else:
            far_ref[...] = total.astype(BF16)


def window_gradient(band, back):
    reps = len(back)
    hidden, rows = back[0].shape

    def kernel(*refs):
        gradient_kernel(reps, *refs)

    return pl.pallas_call(
        kernel,
        in_specs=[pl.BlockSpec(memory_space=pltpu.HBM)] + [pl.BlockSpec(memory_space=pltpu.VMEM)] * reps,
        out_shape=(
            jax.ShapeDtypeStruct((HALF * hidden, rows), F32),
            jax.ShapeDtypeStruct((HALF * hidden, rows), BF16),
            jax.ShapeDtypeStruct((hidden, rows), BF16),
        ),
        scratch_shapes=[pltpu.VMEM(band.shape, BF16), pltpu.SemaphoreType.DMA((SECTIONS,))],
        compiler_params=params(12),
        cost_estimate=cost(GRADIENT_US),
        name="window_gradient",
    )(pltpu.with_memory_space_constraint(band, pltpu.HBM), *back)


def chip_sum_kernel(near_ref, swapped_ref, own_ref, before_ref, after_ref):
    rows = own_ref.shape[0]
    for k, ref in enumerate((own_ref, before_ref, after_ref)):
        at = slice(k * rows, (k + 1) * rows)
        ref[...] = (near_ref[at, :] + swapped_ref[at, :].astype(F32)).astype(ref.dtype)


def chip_sum(near, swapped):
    rows, hidden = near.shape[0] // HALF, near.shape[1]
    return pl.pallas_call(
        chip_sum_kernel,
        out_shape=tuple(jax.ShapeDtypeStruct((rows, hidden), t) for t in (F32, BF16, BF16)),
        compiler_params=params(8),
        cost_estimate=cost(CHIP_SUM_US),
        name="chip_sum",
    )(near, swapped)


def total_kernel(own_ref, after_ref, before_ref, far_ref, out_ref):
    total = own_ref[...]
    for ref in (after_ref, before_ref, far_ref):
        total = total + ref[...].astype(F32)
    out_ref[...] = total.T


def total_gradient(own, after, before, far):
    hidden, rows = own.shape
    return pl.pallas_call(
        total_kernel,
        out_shape=jax.ShapeDtypeStruct((rows, hidden), F32),
        compiler_params=params(8),
        cost_estimate=cost(0.6),
        name="total_gradient",
    )(own, after, before, far)


def spread_kernel(scale, terms_ref, out_ref):
    total = terms_ref[0].astype(F32)
    for k in range(1, terms_ref.shape[0]):
        total = total + terms_ref[k].astype(F32)
    if scale is not None:
        total = total * scale
    total = total.astype(out_ref.dtype)
    for k in range(out_ref.shape[0]):
        out_ref[k] = total


def sum_and_spread(terms, copies, dtype, scale=None):
    def kernel(*refs):
        spread_kernel(scale, *refs)

    return pl.pallas_call(
        kernel,
        out_shape=jax.ShapeDtypeStruct((copies,) + terms.shape[1:], dtype),
        compiler_params=params(8),
        cost_estimate=cost(0.4),
        name="sum_and_spread",
    )(terms)


def on_device(features, block_cols, block_vals, weight, cotangent):
    reps = lax.axis_size("rep")
    group_rows, hidden = features.shape
    side = block_vals.shape[-1]
    blocks_group = group_rows // side
    per_rep = blocks_group // reps
    rows = per_rep * side

    own = own_quarter(features, rows)
    before = chip_shift(own, 1)
    after = chip_shift(own, -1)
    far = far_shift(own)
    band = dense_band(block_cols, block_vals[:, 0], blocks_group, per_rep)
    before, after, far, band = lax.optimization_barrier((before, after, far, band))

    near = jnp.concatenate([own, before, after], axis=0)
    other = core_swap(near)
    parts = to_all(partial_aggregate(band, near, other, far, reps), "rep")

    output_rows, backward, local = dense_layer(parts, weight, cotangent)
    line = lax.axis_size("z")
    plane = lax.axis_size(PLANE)
    node_count = group_rows * lax.axis_size(ROW)
    back = [backward] + [rep_shift(backward, k) for k in range(1, reps)]
    local, back[1] = lax.optimization_barrier((local, back[1]))
    terms = to_all(local.reshape(plane, -1, hidden), PLANE)

    spread = sum_and_spread(terms, line, BF16)
    terms = to_all(spread, "z")
    near_grad, other_grad, far_grad = window_gradient(band, back)
    swapped = core_swap(other_grad)
    from_far = far_shift(far_grad)
    own_grad, before_grad, after_grad = chip_sum(near_grad, swapped)
    from_after = chip_shift(before_grad, -1)
    from_before = chip_shift(after_grad, 1)
    terms, from_far, _, _ = lax.optimization_barrier((terms, from_far, before_grad, after_grad))
    terms = to_all(sum_and_spread(terms, plane, BF16, node_count ** (-0.5)), PLANE)
    grad_features = total_gradient(own_grad, from_after, from_before, from_far)
    terms, grad_features = lax.optimization_barrier((terms, grad_features))
    grad_weight = terms.reshape(hidden, hidden).astype(F32)
    return output_rows, grad_weight, grad_features


def solution(mesh):
    devices = mesh.devices
    split = Mesh(devices.reshape(X_CHIPS, -1, CORES, devices.shape[1]), ROW + ("rep",))
    everywhere = ROW + ("rep",)
    return jax.shard_map(
        on_device,
        mesh=split,
        in_specs=(
            P(ROW, None),
            P(ROW, "rep", None),
            P(ROW, "rep", None, None, None),
            P(),
            P(everywhere, None),
        ),
        out_specs=(P(everywhere, None), P(), P(everywhere, None)),
        check_vma=False,
    )
```

```python
import jax
import jax.numpy as jnp
from jax import lax
from jax.experimental import pallas as pl
from jax.experimental.pallas import tpu as pltpu
from jax.sharding import Mesh
from jax.sharding import PartitionSpec as P

HALF = 3
SECTIONS = 2 * HALF + 1
CORES = 2
X_CHIPS = 4
ROW = ("x", "z", "core")
PLANE = ("x", "core", "rep")
BF16 = jnp.bfloat16
F32 = jnp.float32
PIECE_OF = ((6, 1, 4, 0, 3, 2, 5), (4, 1, 3, 0, 5, 2, 6))
PIECE_CODE = tuple(sum(p << (4 * d) for d, p in enumerate(row)) for row in PIECE_OF)


GRADIENT_US = 2.0
CHIP_SUM_US = 0.5


def cost(us):
    return pl.CostEstimate(flops=0, transcendentals=0, bytes_accessed=int(us * 3.6e6))


def params(mib):
    return pltpu.CompilerParams(vmem_limit_bytes=mib << 20)


def chip_shift(x, by):
    devices = lax.axis_size(ROW)
    by = by * CORES
    return lax.ppermute(x, ROW, [(i, i + by) for i in range(devices) if 0 <= i + by < devices])


def far_shift(x):
    devices = lax.axis_size(ROW)
    pairs = []
    for i in range(devices):
        to = i + HALF if i % CORES else i - HALF
        if 0 <= to < devices:
            pairs.append((i, to))
    return lax.ppermute(x, ROW, pairs)


def core_swap(x):
    return lax.ppermute(x, "core", [(0, 1), (1, 0)])


def rep_shift(x, by):
    devices = lax.axis_size("rep")
    return lax.ppermute(x, "rep", [(i, (i - by) % devices) for i in range(devices)])


def to_all(x, axes):
    return lax.all_to_all(x, axes, 0, 0, tiled=False)


def quarter_kernel(features_ref, out_ref, arrived):
    rows = out_ref.shape[0]
    at = pl.multiple_of(lax.axis_index("rep") * rows, rows)
    fetch = pltpu.make_async_copy(features_ref.at[pl.ds(at, rows), :], out_ref, arrived)
    fetch.start()
    fetch.wait()


def own_quarter(features, rows):
    return pl.pallas_call(
        quarter_kernel,
        in_specs=[pl.BlockSpec(memory_space=pltpu.HBM)],
        out_specs=pl.BlockSpec(memory_space=pltpu.VMEM),
        out_shape=jax.ShapeDtypeStruct((rows, features.shape[1]), features.dtype),
        scratch_shapes=[pltpu.SemaphoreType.DMA(())],
        compiler_params=params(4),
        cost_estimate=cost(0.5),
        name="own_quarter",
    )(pltpu.with_memory_space_constraint(features, pltpu.HBM))


def band_kernel(blocks_group, per_rep, cols_ref, vals_ref, out_ref, held, sums, arrived):
    blocks, slots, side = held.shape[:3]
    columns = sums.shape[0]
    group = lax.axis_index(ROW)
    first = lax.axis_index("rep") * per_rep
    code = jnp.where(lax.axis_index("core") == 0, PIECE_CODE[0], PIECE_CODE[1])

    def fetch(block):
        return pltpu.make_async_copy(vals_ref.at[block], held.at[block], arrived.at[block])

    def rows_of(block):
        return pl.ds(pl.multiple_of(block * side, side), side)

    for block in range(blocks):
        fetch(block).start()

    def step(block, carry):
        fetch(block).wait()
        sums[...] = jnp.zeros_like(sums)
        for s in range(slots):
            column = cols_ref[block, 0, s]
            source = lax.div(column, blocks_group)
            piece = lax.shift_right_logical(code, 4 * (source - group + HALF)) & 15
            at = piece * per_rep + column - source * blocks_group - first
            sums[at] += held[block, s].astype(F32)
        for c in range(columns):
            lanes = slice(c % per_rep * side, (c % per_rep + 1) * side)
            out_ref[c // per_rep, rows_of(block), lanes] = sums[c].astype(BF16)
        return carry

    lax.fori_loop(0, blocks, step, 0)


def dense_band(cols, vals, blocks_group, per_rep):
    blocks, count, side, _ = vals.shape
    columns = SECTIONS * per_rep
    shape = (SECTIONS, blocks * side, per_rep * side)

    def kernel(*refs):
        band_kernel(blocks_group, per_rep, *refs)

    return pl.pallas_call(
        kernel,
        in_specs=[pl.BlockSpec(memory_space=pltpu.SMEM), pl.BlockSpec(memory_space=pltpu.HBM)],
        out_specs=pl.BlockSpec(memory_space=pltpu.VMEM),
        out_shape=jax.ShapeDtypeStruct(shape, BF16),
        scratch_shapes=[
            pltpu.VMEM(vals.shape, BF16),
            pltpu.VMEM((columns, side, side), F32),
            pltpu.SemaphoreType.DMA((blocks,)),
        ],
        compiler_params=params(16),
        cost_estimate=cost(4),
        name="dense_band",
    )(pltpu.with_memory_space_constraint(cols, pltpu.HBM), pltpu.with_memory_space_constraint(vals, pltpu.HBM))


def aggregate_kernel(band_ref, near_ref, other_ref, far_ref, out_ref):
    reps, rows, hidden = out_ref.shape
    for q in range(reps):
        total = jnp.zeros((rows, hidden), F32)
        piece = 0
        for ref in (near_ref, other_ref, far_ref):
            for k in range(ref.shape[0] // rows):
                total = total + jnp.dot(
                    band_ref[piece, q * rows : (q + 1) * rows, :],
                    ref[k * rows : (k + 1) * rows, :],
                    preferred_element_type=F32,
                )
                piece += 1
        out_ref[q] = total.astype(BF16)


def partial_aggregate(band, near, other, far, reps):
    rows, hidden = band.shape[1] // reps, near.shape[1]
    return pl.pallas_call(
        aggregate_kernel,
        out_shape=jax.ShapeDtypeStruct((reps, rows, hidden), BF16),
        compiler_params=params(12),
        cost_estimate=cost(1.5),
        name="partial_aggregate",
    )(band, near, other, far)


def dense_kernel(parts_ref, weight_ref, cotangent_ref, out_ref, back_ref, local_ref):
    reps, rows, hidden = parts_ref.shape
    summed = parts_ref[0].astype(F32)
    for q in range(1, reps):
        summed = summed + parts_ref[q].astype(F32)
    aggregate = summed.astype(BF16)
    preact = jnp.dot(aggregate, weight_ref[...], preferred_element_type=F32)
    sigmoid_pre = 1.0 / (1.0 + jnp.exp(-preact))
    grad_pre = (
        cotangent_ref[...].astype(F32) * sigmoid_pre * (1.0 + preact * (1.0 - sigmoid_pre))
    ).astype(BF16)
    back_ref[...] = lax.dot_general(
        weight_ref[...], grad_pre, (((1,), (1,)), ((), ())), preferred_element_type=F32
    ).astype(BF16)
    local_ref[...] = lax.dot_general(
        aggregate, grad_pre, (((0,), (0,)), ((), ())), preferred_element_type=F32
    )
    out_ref[...] = (preact * sigmoid_pre).astype(BF16)


def dense_layer(parts, weight, cotangent):
    reps, rows, hidden = parts.shape
    return pl.pallas_call(
        dense_kernel,
        out_shape=(
            jax.ShapeDtypeStruct((rows, hidden), BF16),
            jax.ShapeDtypeStruct((hidden, rows), BF16),
            jax.ShapeDtypeStruct((hidden, hidden), F32),
        ),
        compiler_params=params(8),
        cost_estimate=cost(1.3),
        name="dense_layer",
    )(parts, weight, cotangent)


def gradient_kernel(reps, band_ref, *refs):
    near_ref, other_ref, far_ref, held, arrived = refs[reps:]
    hidden, rows = far_ref.shape
    rep = lax.axis_index("rep")

    def fetch(piece):
        return pltpu.make_async_copy(band_ref.at[piece], held.at[piece], arrived.at[piece])

    order = [*range(HALF, 2 * HALF + 1), *range(HALF)]
    for piece in order:
        fetch(piece).start()
    for piece in order:
        fetch(piece).wait()
        total = jnp.zeros((hidden, rows), F32)
        for k in range(reps):
            at = pl.multiple_of(lax.rem(rep + k, reps) * rows, rows)
            total = total + jnp.dot(
                refs[k][...], held[piece, pl.ds(at, rows), :], preferred_element_type=F32
            )
        if piece < HALF:
            near_ref[piece * hidden : (piece + 1) * hidden, :] = total
        elif piece < 2 * HALF:
            other_ref[(piece - HALF) * hidden : (piece - HALF + 1) * hidden, :] = total.astype(BF16)
        else:
            far_ref[...] = total.astype(BF16)


def window_gradient(band, back):
    reps = len(back)
    hidden, rows = back[0].shape

    def kernel(*refs):
        gradient_kernel(reps, *refs)

    return pl.pallas_call(
        kernel,
        in_specs=[pl.BlockSpec(memory_space=pltpu.HBM)] + [pl.BlockSpec(memory_space=pltpu.VMEM)] * reps,
        out_shape=(
            jax.ShapeDtypeStruct((HALF * hidden, rows), F32),
            jax.ShapeDtypeStruct((HALF * hidden, rows), BF16),
            jax.ShapeDtypeStruct((hidden, rows), BF16),
        ),
        scratch_shapes=[pltpu.VMEM(band.shape, BF16), pltpu.SemaphoreType.DMA((SECTIONS,))],
        compiler_params=params(12),
        cost_estimate=cost(GRADIENT_US),
        name="window_gradient",
    )(pltpu.with_memory_space_constraint(band, pltpu.HBM), *back)


def chip_sum_kernel(near_ref, swapped_ref, own_ref, before_ref, after_ref):
    rows = own_ref.shape[0]
    for k, ref in enumerate((own_ref, before_ref, after_ref)):
        at = slice(k * rows, (k + 1) * rows)
        ref[...] = (near_ref[at, :] + swapped_ref[at, :].astype(F32)).astype(ref.dtype)


def chip_sum(near, swapped):
    rows, hidden = near.shape[0] // HALF, near.shape[1]
    return pl.pallas_call(
        chip_sum_kernel,
        out_shape=tuple(jax.ShapeDtypeStruct((rows, hidden), t) for t in (F32, BF16, BF16)),
        compiler_params=params(8),
        cost_estimate=cost(CHIP_SUM_US),
        name="chip_sum",
    )(near, swapped)


def total_kernel(own_ref, after_ref, before_ref, far_ref, out_ref):
    total = own_ref[...]
    for ref in (after_ref, before_ref, far_ref):
        total = total + ref[...].astype(F32)
    out_ref[...] = total.T


def total_gradient(own, after, before, far):
    hidden, rows = own.shape
    return pl.pallas_call(
        total_kernel,
        out_shape=jax.ShapeDtypeStruct((rows, hidden), F32),
        compiler_params=params(8),
        cost_estimate=cost(0.6),
        name="total_gradient",
    )(own, after, before, far)


def spread_kernel(scale, terms_ref, out_ref):
    total = terms_ref[0].astype(F32)
    for k in range(1, terms_ref.shape[0]):
        total = total + terms_ref[k].astype(F32)
    if scale is not None:
        total = total * scale
    total = total.astype(out_ref.dtype)
    for k in range(out_ref.shape[0]):
        out_ref[k] = total


def sum_and_spread(terms, copies, dtype, scale=None):
    def kernel(*refs):
        spread_kernel(scale, *refs)

    return pl.pallas_call(
        kernel,
        out_shape=jax.ShapeDtypeStruct((copies,) + terms.shape[1:], dtype),
        compiler_params=params(8),
        cost_estimate=cost(0.4),
        name="sum_and_spread",
    )(terms)


def on_device(features, block_cols, block_vals, weight, cotangent):
    reps = lax.axis_size("rep")
    group_rows, hidden = features.shape
    side = block_vals.shape[-1]
    blocks_group = group_rows // side
    per_rep = blocks_group // reps
    rows = per_rep * side

    own = own_quarter(features, rows)
    before = chip_shift(own, 1)
    after = chip_shift(own, -1)
    far = far_shift(own)
    band = dense_band(block_cols, block_vals[:, 0], blocks_group, per_rep)
    far, after, before, band = lax.optimization_barrier((far, after, before, band))

    near = jnp.concatenate([own, before, after], axis=0)
    other = core_swap(near)
    parts = to_all(partial_aggregate(band, near, other, far, reps), "rep")

    output_rows, backward, local = dense_layer(parts, weight, cotangent)
    line = lax.axis_size("z")
    plane = lax.axis_size(PLANE)
    node_count = group_rows * lax.axis_size(ROW)
    back = [backward] + [rep_shift(backward, k) for k in range(1, reps)]
    local, back[1] = lax.optimization_barrier((local, back[1]))
    terms = to_all(local.reshape(plane, -1, hidden), PLANE)

    spread = sum_and_spread(terms, line, BF16)
    terms = to_all(spread, "z")
    near_grad, other_grad, far_grad = window_gradient(band, back)
    swapped = core_swap(other_grad)
    from_far = far_shift(far_grad)
    own_grad, before_grad, after_grad = chip_sum(near_grad, swapped)
    from_after = chip_shift(before_grad, -1)
    from_before = chip_shift(after_grad, 1)
    terms, from_far, _, _ = lax.optimization_barrier((terms, from_far, before_grad, after_grad))
    terms = to_all(sum_and_spread(terms, plane, BF16, node_count ** (-0.5)), PLANE)
    grad_features = total_gradient(own_grad, from_after, from_before, from_far)
    terms, grad_features = lax.optimization_barrier((terms, grad_features))
    grad_weight = terms.reshape(hidden, hidden).astype(F32)
    return output_rows, grad_weight, grad_features


def solution(mesh):
    devices = mesh.devices
    split = Mesh(devices.reshape(X_CHIPS, -1, CORES, devices.shape[1]), ROW + ("rep",))
    everywhere = ROW + ("rep",)
    return jax.shard_map(
        on_device,
        mesh=split,
        in_specs=(
            P(ROW, None),
            P(ROW, "rep", None),
            P(ROW, "rep", None, None, None),
            P(),
            P(everywhere, None),
        ),
        out_specs=(P(everywhere, None), P(), P(everywhere, None)),
        check_vma=False,
    )
```

```python
import jax
import jax.numpy as jnp
from jax import lax
from jax.experimental import pallas as pl
from jax.experimental.pallas import tpu as pltpu
from jax.sharding import Mesh
from jax.sharding import PartitionSpec as P

HALF = 3
SECTIONS = 2 * HALF + 1
CORES = 2
X_CHIPS = 4
ROW = ("x", "z", "core")
PLANE = ("x", "core", "rep")
BF16 = jnp.bfloat16
F32 = jnp.float32
PIECE_OF = ((6, 1, 4, 0, 3, 2, 5), (4, 1, 3, 0, 5, 2, 6))
PIECE_CODE = tuple(sum(p << (4 * d) for d, p in enumerate(row)) for row in PIECE_OF)


GRADIENT_US = 2.0
CHIP_SUM_US = 0.5


def cost(us):
    return pl.CostEstimate(flops=0, transcendentals=0, bytes_accessed=int(us * 3.6e6))


def params(mib):
    return pltpu.CompilerParams(vmem_limit_bytes=mib << 20)


def chip_shift(x, by):
    devices = lax.axis_size(ROW)
    by = by * CORES
    return lax.ppermute(x, ROW, [(i, i + by) for i in range(devices) if 0 <= i + by < devices])


def far_shift(x):
    devices = lax.axis_size(ROW)
    pairs = []
    for i in range(devices):
        to = i + HALF if i % CORES else i - HALF
        if 0 <= to < devices:
            pairs.append((i, to))
    return lax.ppermute(x, ROW, pairs)


def core_swap(x):
    return lax.ppermute(x, "core", [(0, 1), (1, 0)])


def rep_shift(x, by):
    devices = lax.axis_size("rep")
    return lax.ppermute(x, "rep", [(i, (i - by) % devices) for i in range(devices)])


def to_all(x, axes):
    return lax.all_to_all(x, axes, 0, 0, tiled=False)


def quarter_kernel(features_ref, out_ref, arrived):
    rows = out_ref.shape[0]
    at = pl.multiple_of(lax.axis_index("rep") * rows, rows)
    fetch = pltpu.make_async_copy(features_ref.at[pl.ds(at, rows), :], out_ref, arrived)
    fetch.start()
    fetch.wait()


def own_quarter(features, rows):
    return pl.pallas_call(
        quarter_kernel,
        in_specs=[pl.BlockSpec(memory_space=pltpu.HBM)],
        out_specs=pl.BlockSpec(memory_space=pltpu.VMEM),
        out_shape=jax.ShapeDtypeStruct((rows, features.shape[1]), features.dtype),
        scratch_shapes=[pltpu.SemaphoreType.DMA(())],
        compiler_params=params(4),
        cost_estimate=cost(0.5),
        name="own_quarter",
    )(pltpu.with_memory_space_constraint(features, pltpu.HBM))


def band_kernel(blocks_group, per_rep, cols_ref, vals_ref, out_ref, held, sums, arrived):
    blocks, slots, side = held.shape[:3]
    columns = sums.shape[0]
    group = lax.axis_index(ROW)
    first = lax.axis_index("rep") * per_rep
    code = jnp.where(lax.axis_index("core") == 0, PIECE_CODE[0], PIECE_CODE[1])

    def fetch(block):
        return pltpu.make_async_copy(vals_ref.at[block], held.at[block], arrived.at[block])

    def rows_of(block):
        return pl.ds(pl.multiple_of(block * side, side), side)

    for block in range(blocks):
        fetch(block).start()

    def step(block, carry):
        fetch(block).wait()
        sums[...] = jnp.zeros_like(sums)
        for s in range(slots):
            column = cols_ref[block, 0, s]
            source = lax.div(column, blocks_group)
            piece = lax.shift_right_logical(code, 4 * (source - group + HALF)) & 15
            at = piece * per_rep + column - source * blocks_group - first
            sums[at] += held[block, s].astype(F32)
        for c in range(columns):
            lanes = slice(c % per_rep * side, (c % per_rep + 1) * side)
            out_ref[c // per_rep, rows_of(block), lanes] = sums[c].astype(BF16)
        return carry

    lax.fori_loop(0, blocks, step, 0)


def dense_band(cols, vals, blocks_group, per_rep):
    blocks, count, side, _ = vals.shape
    columns = SECTIONS * per_rep
    shape = (SECTIONS, blocks * side, per_rep * side)

    def kernel(*refs):
        band_kernel(blocks_group, per_rep, *refs)

    return pl.pallas_call(
        kernel,
        in_specs=[pl.BlockSpec(memory_space=pltpu.SMEM), pl.BlockSpec(memory_space=pltpu.HBM)],
        out_specs=pl.BlockSpec(memory_space=pltpu.VMEM),
        out_shape=jax.ShapeDtypeStruct(shape, BF16),
        scratch_shapes=[
            pltpu.VMEM(vals.shape, BF16),
            pltpu.VMEM((columns, side, side), F32),
            pltpu.SemaphoreType.DMA((blocks,)),
        ],
        compiler_params=params(16),
        cost_estimate=cost(4),
        name="dense_band",
    )(pltpu.with_memory_space_constraint(cols, pltpu.HBM), pltpu.with_memory_space_constraint(vals, pltpu.HBM))


def aggregate_kernel(band_ref, near_ref, other_ref, far_ref, out_ref):
    reps, rows, hidden = out_ref.shape
    for q in range(reps):
        total = jnp.zeros((rows, hidden), F32)
        piece = 0
        for ref in (near_ref, other_ref, far_ref):
            for k in range(ref.shape[0] // rows):
                total = total + jnp.dot(
                    band_ref[piece, q * rows : (q + 1) * rows, :],
                    ref[k * rows : (k + 1) * rows, :],
                    preferred_element_type=F32,
                )
                piece += 1
        out_ref[q] = total.astype(BF16)


def partial_aggregate(band, near, other, far, reps):
    rows, hidden = band.shape[1] // reps, near.shape[1]
    return pl.pallas_call(
        aggregate_kernel,
        out_shape=jax.ShapeDtypeStruct((reps, rows, hidden), BF16),
        compiler_params=params(12),
        cost_estimate=cost(1.5),
        name="partial_aggregate",
    )(band, near, other, far)


def dense_kernel(parts_ref, weight_ref, cotangent_ref, out_ref, back_ref, local_ref):
    reps, rows, hidden = parts_ref.shape
    summed = parts_ref[0].astype(F32)
    for q in range(1, reps):
        summed = summed + parts_ref[q].astype(F32)
    aggregate = summed.astype(BF16)
    preact = jnp.dot(aggregate, weight_ref[...], preferred_element_type=F32)
    sigmoid_pre = 1.0 / (1.0 + jnp.exp(-preact))
    grad_pre = (
        cotangent_ref[...].astype(F32) * sigmoid_pre * (1.0 + preact * (1.0 - sigmoid_pre))
    ).astype(BF16)
    back_ref[...] = lax.dot_general(
        weight_ref[...], grad_pre, (((1,), (1,)), ((), ())), preferred_element_type=F32
    ).astype(BF16)
    local_ref[...] = lax.dot_general(
        aggregate, grad_pre, (((0,), (0,)), ((), ())), preferred_element_type=F32
    )
    out_ref[...] = (preact * sigmoid_pre).astype(BF16)


def dense_layer(parts, weight, cotangent):
    reps, rows, hidden = parts.shape
    return pl.pallas_call(
        dense_kernel,
        out_shape=(
            jax.ShapeDtypeStruct((rows, hidden), BF16),
            jax.ShapeDtypeStruct((hidden, rows), BF16),
            jax.ShapeDtypeStruct((hidden, hidden), F32),
        ),
        compiler_params=params(8),
        cost_estimate=cost(1.3),
        name="dense_layer",
    )(parts, weight, cotangent)


def gradient_kernel(reps, band_ref, *refs):
    near_ref, other_ref, far_ref, held, arrived = refs[reps:]
    hidden, rows = far_ref.shape
    rep = lax.axis_index("rep")

    def fetch(piece):
        return pltpu.make_async_copy(band_ref.at[piece], held.at[piece], arrived.at[piece])

    order = [*range(HALF, 2 * HALF + 1), *range(HALF)]
    for piece in order:
        fetch(piece).start()
    for piece in order:
        fetch(piece).wait()
        total = jnp.zeros((hidden, rows), F32)
        for k in range(reps):
            at = pl.multiple_of(lax.rem(rep + k, reps) * rows, rows)
            total = total + jnp.dot(
                refs[k][...], held[piece, pl.ds(at, rows), :], preferred_element_type=F32
            )
        if piece < HALF:
            near_ref[piece * hidden : (piece + 1) * hidden, :] = total
        elif piece < 2 * HALF:
            other_ref[(piece - HALF) * hidden : (piece - HALF + 1) * hidden, :] = total.astype(BF16)
        else:
            far_ref[...] = total.astype(BF16)


def window_gradient(band, back):
    reps = len(back)
    hidden, rows = back[0].shape

    def kernel(*refs):
        gradient_kernel(reps, *refs)

    return pl.pallas_call(
        kernel,
        in_specs=[pl.BlockSpec(memory_space=pltpu.HBM)] + [pl.BlockSpec(memory_space=pltpu.VMEM)] * reps,
        out_shape=(
            jax.ShapeDtypeStruct((HALF * hidden, rows), F32),
            jax.ShapeDtypeStruct((HALF * hidden, rows), BF16),
            jax.ShapeDtypeStruct((hidden, rows), BF16),
        ),
        scratch_shapes=[pltpu.VMEM(band.shape, BF16), pltpu.SemaphoreType.DMA((SECTIONS,))],
        compiler_params=params(12),
        cost_estimate=cost(GRADIENT_US),
        name="window_gradient",
    )(pltpu.with_memory_space_constraint(band, pltpu.HBM), *back)


def chip_sum_kernel(near_ref, swapped_ref, own_ref, before_ref, after_ref):
    rows = own_ref.shape[0]
    for k, ref in enumerate((own_ref, before_ref, after_ref)):
        at = slice(k * rows, (k + 1) * rows)
        ref[...] = (near_ref[at, :] + swapped_ref[at, :].astype(F32)).astype(ref.dtype)


def chip_sum(near, swapped):
    rows, hidden = near.shape[0] // HALF, near.shape[1]
    return pl.pallas_call(
        chip_sum_kernel,
        out_shape=tuple(jax.ShapeDtypeStruct((rows, hidden), t) for t in (F32, BF16, BF16)),
        compiler_params=params(8),
        cost_estimate=cost(CHIP_SUM_US),
        name="chip_sum",
    )(near, swapped)


def total_kernel(own_ref, after_ref, before_ref, far_ref, out_ref):
    total = own_ref[...]
    for ref in (after_ref, before_ref, far_ref):
        total = total + ref[...].astype(F32)
    out_ref[...] = total.T


def total_gradient(own, after, before, far):
    hidden, rows = own.shape
    return pl.pallas_call(
        total_kernel,
        out_shape=jax.ShapeDtypeStruct((rows, hidden), F32),
        compiler_params=params(8),
        cost_estimate=cost(0.6),
        name="total_gradient",
    )(own, after, before, far)


def spread_kernel(scale, terms_ref, out_ref):
    total = terms_ref[0].astype(F32)
    for k in range(1, terms_ref.shape[0]):
        total = total + terms_ref[k].astype(F32)
    if scale is not None:
        total = total * scale
    total = total.astype(out_ref.dtype)
    for k in range(out_ref.shape[0]):
        out_ref[k] = total


def sum_and_spread(terms, copies, dtype, scale=None):
    def kernel(*refs):
        spread_kernel(scale, *refs)

    return pl.pallas_call(
        kernel,
        out_shape=jax.ShapeDtypeStruct((copies,) + terms.shape[1:], dtype),
        compiler_params=params(8),
        cost_estimate=cost(0.4),
        name="sum_and_spread",
    )(terms)


def on_device(features, block_cols, block_vals, weight, cotangent):
    reps = lax.axis_size("rep")
    group_rows, hidden = features.shape
    side = block_vals.shape[-1]
    blocks_group = group_rows // side
    per_rep = blocks_group // reps
    rows = per_rep * side

    own = own_quarter(features, rows)
    before = chip_shift(own, 1)
    after = chip_shift(own, -1)
    far = far_shift(own)
    band = dense_band(block_cols, block_vals[:, 0], blocks_group, per_rep)
    far, after, before, band = lax.optimization_barrier((far, after, before, band))

    near = jnp.concatenate([own, before, after], axis=0)
    other = core_swap(near)
    parts = to_all(partial_aggregate(band, near, other, far, reps), "rep")

    output_rows, backward, local = dense_layer(parts, weight, cotangent)
    line = lax.axis_size("z")
    plane = lax.axis_size(PLANE)
    node_count = group_rows * lax.axis_size(ROW)
    back = [backward] + [rep_shift(backward, k) for k in range(1, reps)]
    terms = to_all(local.reshape(plane, -1, hidden), PLANE)

    spread = sum_and_spread(terms, line, F32)
    terms = to_all(spread, "z")
    band, _ = lax.optimization_barrier((band, spread))
    near_grad, other_grad, far_grad = window_gradient(band, back)
    swapped = core_swap(other_grad)
    from_far = far_shift(far_grad)
    own_grad, before_grad, after_grad = chip_sum(near_grad, swapped)
    from_after = chip_shift(before_grad, -1)
    terms, from_far, _ = lax.optimization_barrier((terms, from_far, before_grad))
    spread = sum_and_spread(terms, plane, BF16, node_count ** (-0.5))
    terms = to_all(spread, PLANE)
    after_grad, _ = lax.optimization_barrier((after_grad, spread))
    from_before = chip_shift(after_grad, 1)
    grad_features = total_gradient(own_grad, from_after, from_before, from_far)
    grad_weight = terms.reshape(hidden, hidden).astype(F32)
    return output_rows, grad_weight, grad_features


def solution(mesh):
    devices = mesh.devices
    split = Mesh(devices.reshape(X_CHIPS, -1, CORES, devices.shape[1]), ROW + ("rep",))
    everywhere = ROW + ("rep",)
    return jax.shard_map(
        on_device,
        mesh=split,
        in_specs=(
            P(ROW, None),
            P(ROW, "rep", None),
            P(ROW, "rep", None, None, None),
            P(),
            P(everywhere, None),
        ),
        out_specs=(P(everywhere, None), P(), P(everywhere, None)),
        check_vma=False,
    )
```

```python
import jax
import jax.numpy as jnp
from jax import lax
from jax.experimental import pallas as pl
from jax.experimental.pallas import tpu as pltpu
from jax.sharding import Mesh
from jax.sharding import PartitionSpec as P

HALF = 3
SECTIONS = 2 * HALF + 1
CORES = 2
X_CHIPS = 4
ROW = ("x", "z", "core")
PLANE = ("x", "core", "rep")
BF16 = jnp.bfloat16
F32 = jnp.float32
PIECE_OF = ((6, 1, 4, 0, 3, 2, 5), (4, 1, 3, 0, 5, 2, 6))
PIECE_CODE = tuple(sum(p << (4 * d) for d, p in enumerate(row)) for row in PIECE_OF)


GRADIENT_US = 2.0
CHIP_SUM_US = 0.5


def cost(us):
    return pl.CostEstimate(flops=0, transcendentals=0, bytes_accessed=int(us * 3.6e6))


def params(mib):
    return pltpu.CompilerParams(vmem_limit_bytes=mib << 20)


def chip_shift(x, by):
    devices = lax.axis_size(ROW)
    by = by * CORES
    return lax.ppermute(x, ROW, [(i, i + by) for i in range(devices) if 0 <= i + by < devices])


def far_shift(x):
    devices = lax.axis_size(ROW)
    pairs = []
    for i in range(devices):
        to = i + HALF if i % CORES else i - HALF
        if 0 <= to < devices:
            pairs.append((i, to))
    return lax.ppermute(x, ROW, pairs)


def core_swap(x):
    return lax.ppermute(x, "core", [(0, 1), (1, 0)])


def rep_shift(x, by):
    devices = lax.axis_size("rep")
    return lax.ppermute(x, "rep", [(i, (i - by) % devices) for i in range(devices)])


def to_all(x, axes):
    return lax.all_to_all(x, axes, 0, 0, tiled=False)


def quarter_kernel(features_ref, out_ref, arrived):
    rows = out_ref.shape[0]
    at = pl.multiple_of(lax.axis_index("rep") * rows, rows)
    fetch = pltpu.make_async_copy(features_ref.at[pl.ds(at, rows), :], out_ref, arrived)
    fetch.start()
    fetch.wait()


def own_quarter(features, rows):
    return pl.pallas_call(
        quarter_kernel,
        in_specs=[pl.BlockSpec(memory_space=pltpu.HBM)],
        out_specs=pl.BlockSpec(memory_space=pltpu.VMEM),
        out_shape=jax.ShapeDtypeStruct((rows, features.shape[1]), features.dtype),
        scratch_shapes=[pltpu.SemaphoreType.DMA(())],
        compiler_params=params(4),
        cost_estimate=cost(0.5),
        name="own_quarter",
    )(pltpu.with_memory_space_constraint(features, pltpu.HBM))


def band_kernel(blocks_group, per_rep, cols_ref, vals_ref, out_ref, held, sums, arrived):
    blocks, slots, side = held.shape[:3]
    columns = sums.shape[0]
    group = lax.axis_index(ROW)
    first = lax.axis_index("rep") * per_rep
    code = jnp.where(lax.axis_index("core") == 0, PIECE_CODE[0], PIECE_CODE[1])

    def fetch(block):
        return pltpu.make_async_copy(vals_ref.at[block], held.at[block], arrived.at[block])

    def rows_of(block):
        return pl.ds(pl.multiple_of(block * side, side), side)

    for block in range(blocks):
        fetch(block).start()

    def step(block, carry):
        fetch(block).wait()
        sums[...] = jnp.zeros_like(sums)
        for s in range(slots):
            column = cols_ref[block, 0, s]
            source = lax.div(column, blocks_group)
            piece = lax.shift_right_logical(code, 4 * (source - group + HALF)) & 15
            at = piece * per_rep + column - source * blocks_group - first
            sums[at] += held[block, s].astype(F32)
        for c in range(columns):
            lanes = slice(c % per_rep * side, (c % per_rep + 1) * side)
            out_ref[c // per_rep, rows_of(block), lanes] = sums[c].astype(BF16)
        return carry

    lax.fori_loop(0, blocks, step, 0)


def dense_band(cols, vals, blocks_group, per_rep):
    blocks, count, side, _ = vals.shape
    columns = SECTIONS * per_rep
    shape = (SECTIONS, blocks * side, per_rep * side)

    def kernel(*refs):
        band_kernel(blocks_group, per_rep, *refs)

    return pl.pallas_call(
        kernel,
        in_specs=[pl.BlockSpec(memory_space=pltpu.SMEM), pl.BlockSpec(memory_space=pltpu.HBM)],
        out_specs=pl.BlockSpec(memory_space=pltpu.VMEM),
        out_shape=jax.ShapeDtypeStruct(shape, BF16),
        scratch_shapes=[
            pltpu.VMEM(vals.shape, BF16),
            pltpu.VMEM((columns, side, side), F32),
            pltpu.SemaphoreType.DMA((blocks,)),
        ],
        compiler_params=params(16),
        cost_estimate=cost(4),
        name="dense_band",
    )(pltpu.with_memory_space_constraint(cols, pltpu.HBM), pltpu.with_memory_space_constraint(vals, pltpu.HBM))


def aggregate_kernel(band_ref, near_ref, other_ref, far_ref, out_ref):
    reps, rows, hidden = out_ref.shape
    for q in range(reps):
        total = jnp.zeros((rows, hidden), F32)
        piece = 0
        for ref in (near_ref, other_ref, far_ref):
            for k in range(ref.shape[0] // rows):
                total = total + jnp.dot(
                    band_ref[piece, q * rows : (q + 1) * rows, :],
                    ref[k * rows : (k + 1) * rows, :],
                    preferred_element_type=F32,
                )
                piece += 1
        out_ref[q] = total.astype(BF16)


def partial_aggregate(band, near, other, far, reps):
    rows, hidden = band.shape[1] // reps, near.shape[1]
    return pl.pallas_call(
        aggregate_kernel,
        out_shape=jax.ShapeDtypeStruct((reps, rows, hidden), BF16),
        compiler_params=params(12),
        cost_estimate=cost(1.5),
        name="partial_aggregate",
    )(band, near, other, far)


def dense_kernel(parts_ref, weight_ref, cotangent_ref, out_ref, back_ref, local_ref):
    reps, rows, hidden = parts_ref.shape
    summed = parts_ref[0].astype(F32)
    for q in range(1, reps):
        summed = summed + parts_ref[q].astype(F32)
    aggregate = summed.astype(BF16)
    preact = jnp.dot(aggregate, weight_ref[...], preferred_element_type=F32)
    sigmoid_pre = 1.0 / (1.0 + jnp.exp(-preact))
    grad_pre = (
        cotangent_ref[...].astype(F32) * sigmoid_pre * (1.0 + preact * (1.0 - sigmoid_pre))
    ).astype(BF16)
    back_ref[...] = lax.dot_general(
        weight_ref[...], grad_pre, (((1,), (1,)), ((), ())), preferred_element_type=F32
    ).astype(BF16)
    local_ref[...] = lax.dot_general(
        aggregate, grad_pre, (((0,), (0,)), ((), ())), preferred_element_type=F32
    )
    out_ref[...] = (preact * sigmoid_pre).astype(BF16)


def dense_layer(parts, weight, cotangent):
    reps, rows, hidden = parts.shape
    return pl.pallas_call(
        dense_kernel,
        out_shape=(
            jax.ShapeDtypeStruct((rows, hidden), BF16),
            jax.ShapeDtypeStruct((hidden, rows), BF16),
            jax.ShapeDtypeStruct((hidden, hidden), F32),
        ),
        compiler_params=params(8),
        cost_estimate=cost(1.3),
        name="dense_layer",
    )(parts, weight, cotangent)


def gradient_kernel(reps, band_ref, *refs):
    near_ref, other_ref, far_ref, held, arrived = refs[reps:]
    hidden, rows = far_ref.shape
    rep = lax.axis_index("rep")

    def fetch(piece):
        return pltpu.make_async_copy(band_ref.at[piece], held.at[piece], arrived.at[piece])

    order = [*range(HALF, 2 * HALF + 1), *range(HALF)]
    for piece in order:
        fetch(piece).start()
    for piece in order:
        fetch(piece).wait()
        total = jnp.zeros((hidden, rows), F32)
        for k in range(reps):
            at = pl.multiple_of(lax.rem(rep + k, reps) * rows, rows)
            total = total + jnp.dot(
                refs[k][...], held[piece, pl.ds(at, rows), :], preferred_element_type=F32
            )
        if piece < HALF:
            near_ref[piece * hidden : (piece + 1) * hidden, :] = total
        elif piece < 2 * HALF:
            other_ref[(piece - HALF) * hidden : (piece - HALF + 1) * hidden, :] = total.astype(BF16)
        else:
            far_ref[...] = total.astype(BF16)


def window_gradient(band, back):
    reps = len(back)
    hidden, rows = back[0].shape

    def kernel(*refs):
        gradient_kernel(reps, *refs)

    return pl.pallas_call(
        kernel,
        in_specs=[pl.BlockSpec(memory_space=pltpu.HBM)] + [pl.BlockSpec(memory_space=pltpu.VMEM)] * reps,
        out_shape=(
            jax.ShapeDtypeStruct((HALF * hidden, rows), F32),
            jax.ShapeDtypeStruct((HALF * hidden, rows), BF16),
            jax.ShapeDtypeStruct((hidden, rows), BF16),
        ),
        scratch_shapes=[pltpu.VMEM(band.shape, BF16), pltpu.SemaphoreType.DMA((SECTIONS,))],
        compiler_params=params(12),
        cost_estimate=cost(GRADIENT_US),
        name="window_gradient",
    )(pltpu.with_memory_space_constraint(band, pltpu.HBM), *back)


def chip_sum_kernel(near_ref, swapped_ref, own_ref, before_ref, after_ref):
    rows = own_ref.shape[0]
    for k, ref in enumerate((own_ref, before_ref, after_ref)):
        at = slice(k * rows, (k + 1) * rows)
        ref[...] = (near_ref[at, :] + swapped_ref[at, :].astype(F32)).astype(ref.dtype)


def chip_sum(near, swapped):
    rows, hidden = near.shape[0] // HALF, near.shape[1]
    return pl.pallas_call(
        chip_sum_kernel,
        out_shape=tuple(jax.ShapeDtypeStruct((rows, hidden), t) for t in (F32, BF16, BF16)),
        compiler_params=params(8),
        cost_estimate=cost(CHIP_SUM_US),
        name="chip_sum",
    )(near, swapped)


def total_kernel(own_ref, after_ref, before_ref, far_ref, out_ref):
    total = own_ref[...]
    for ref in (after_ref, before_ref, far_ref):
        total = total + ref[...].astype(F32)
    out_ref[...] = total.T


def total_gradient(own, after, before, far):
    hidden, rows = own.shape
    return pl.pallas_call(
        total_kernel,
        out_shape=jax.ShapeDtypeStruct((rows, hidden), F32),
        compiler_params=params(8),
        cost_estimate=cost(0.6),
        name="total_gradient",
    )(own, after, before, far)


def spread_kernel(scale, terms_ref, out_ref):
    total = terms_ref[0].astype(F32)
    for k in range(1, terms_ref.shape[0]):
        total = total + terms_ref[k].astype(F32)
    if scale is not None:
        total = total * scale
    total = total.astype(out_ref.dtype)
    for k in range(out_ref.shape[0]):
        out_ref[k] = total


def sum_and_spread(terms, copies, dtype, scale=None):
    def kernel(*refs):
        spread_kernel(scale, *refs)

    return pl.pallas_call(
        kernel,
        out_shape=jax.ShapeDtypeStruct((copies,) + terms.shape[1:], dtype),
        compiler_params=params(8),
        cost_estimate=cost(0.4),
        name="sum_and_spread",
    )(terms)


def on_device(features, block_cols, block_vals, weight, cotangent):
    reps = lax.axis_size("rep")
    group_rows, hidden = features.shape
    side = block_vals.shape[-1]
    blocks_group = group_rows // side
    per_rep = blocks_group // reps
    rows = per_rep * side

    own = own_quarter(features, rows)
    before = chip_shift(own, 1)
    after = chip_shift(own, -1)
    far = far_shift(own)
    band = dense_band(block_cols, block_vals[:, 0], blocks_group, per_rep)
    far, after, before, band = lax.optimization_barrier((far, after, before, band))

    near = jnp.concatenate([own, before, after], axis=0)
    other = core_swap(near)
    parts = to_all(partial_aggregate(band, near, other, far, reps), "rep")

    output_rows, backward, local = dense_layer(parts, weight, cotangent)
    line = lax.axis_size("z")
    plane = lax.axis_size(PLANE)
    node_count = group_rows * lax.axis_size(ROW)
    back = [backward] + [rep_shift(backward, k) for k in range(1, reps)]
    terms = to_all(local.reshape(plane, -1, hidden), PLANE)

    spread = sum_and_spread(terms, line, F32)
    terms = to_all(spread, "z")
    band, _ = lax.optimization_barrier((band, spread))
    near_grad, other_grad, far_grad = window_gradient(band, back)
    swapped = core_swap(other_grad)
    from_far = far_shift(far_grad)
    own_grad, before_grad, after_grad = chip_sum(near_grad, swapped)
    from_after = chip_shift(before_grad, -1)
    terms, _ = lax.optimization_barrier((terms, before_grad))
    spread = sum_and_spread(terms, plane, BF16, node_count ** (-0.5))
    terms = to_all(spread, PLANE)
    after_grad, _ = lax.optimization_barrier((after_grad, spread))
    from_before = chip_shift(after_grad, 1)
    grad_features = total_gradient(own_grad, from_after, from_before, from_far)
    terms, from_far, from_after = lax.optimization_barrier((terms, from_far, from_after))
    grad_weight = terms.reshape(hidden, hidden).astype(F32)
    return output_rows, grad_weight, grad_features


def solution(mesh):
    devices = mesh.devices
    split = Mesh(devices.reshape(X_CHIPS, -1, CORES, devices.shape[1]), ROW + ("rep",))
    everywhere = ROW + ("rep",)
    return jax.shard_map(
        on_device,
        mesh=split,
        in_specs=(
            P(ROW, None),
            P(ROW, "rep", None),
            P(ROW, "rep", None, None, None),
            P(),
            P(everywhere, None),
        ),
        out_specs=(P(everywhere, None), P(), P(everywhere, None)),
        check_vma=False,
    )
```

```python
import jax
import jax.numpy as jnp
from jax import lax
from jax.experimental import pallas as pl
from jax.experimental.pallas import tpu as pltpu
from jax.sharding import Mesh
from jax.sharding import PartitionSpec as P

HALF = 3
SECTIONS = 2 * HALF + 1
CORES = 2
X_CHIPS = 4
ROW = ("x", "z", "core")
PLANE = ("x", "core", "rep")
BF16 = jnp.bfloat16
F32 = jnp.float32
PIECE_OF = ((6, 1, 4, 0, 3, 2, 5), (4, 1, 3, 0, 5, 2, 6))
PIECE_CODE = tuple(sum(p << (4 * d) for d, p in enumerate(row)) for row in PIECE_OF)


GRADIENT_US = 2.0
CHIP_SUM_US = 0.5


def cost(us):
    return pl.CostEstimate(flops=0, transcendentals=0, bytes_accessed=int(us * 3.6e6))


def params(mib):
    return pltpu.CompilerParams(vmem_limit_bytes=mib << 20)


def chip_shift(x, by):
    devices = lax.axis_size(ROW)
    by = by * CORES
    return lax.ppermute(x, ROW, [(i, i + by) for i in range(devices) if 0 <= i + by < devices])


def far_shift(x):
    devices = lax.axis_size(ROW)
    pairs = []
    for i in range(devices):
        to = i + HALF if i % CORES else i - HALF
        if 0 <= to < devices:
            pairs.append((i, to))
    return lax.ppermute(x, ROW, pairs)


def core_swap(x):
    return lax.ppermute(x, "core", [(0, 1), (1, 0)])


def rep_shift(x, by):
    devices = lax.axis_size("rep")
    return lax.ppermute(x, "rep", [(i, (i - by) % devices) for i in range(devices)])


def to_all(x, axes):
    return lax.all_to_all(x, axes, 0, 0, tiled=False)


def quarter_kernel(features_ref, out_ref, arrived):
    rows = out_ref.shape[0]
    at = pl.multiple_of(lax.axis_index("rep") * rows, rows)
    fetch = pltpu.make_async_copy(features_ref.at[pl.ds(at, rows), :], out_ref, arrived)
    fetch.start()
    fetch.wait()


def own_quarter(features, rows):
    return pl.pallas_call(
        quarter_kernel,
        in_specs=[pl.BlockSpec(memory_space=pltpu.HBM)],
        out_specs=pl.BlockSpec(memory_space=pltpu.VMEM),
        out_shape=jax.ShapeDtypeStruct((rows, features.shape[1]), features.dtype),
        scratch_shapes=[pltpu.SemaphoreType.DMA(())],
        compiler_params=params(4),
        cost_estimate=cost(0.5),
        name="own_quarter",
    )(pltpu.with_memory_space_constraint(features, pltpu.HBM))


def band_kernel(blocks_group, per_rep, cols_ref, vals_ref, out_ref, held, sums, arrived):
    blocks, slots, side = held.shape[:3]
    columns = sums.shape[0]
    group = lax.axis_index(ROW)
    first = lax.axis_index("rep") * per_rep
    code = jnp.where(lax.axis_index("core") == 0, PIECE_CODE[0], PIECE_CODE[1])

    def fetch(block):
        return pltpu.make_async_copy(vals_ref.at[block], held.at[block], arrived.at[block])

    def rows_of(block):
        return pl.ds(pl.multiple_of(block * side, side), side)

    for block in range(blocks):
        fetch(block).start()

    def step(block, carry):
        fetch(block).wait()
        sums[...] = jnp.zeros_like(sums)
        for s in range(slots):
            column = cols_ref[block, 0, s]
            source = lax.div(column, blocks_group)
            piece = lax.shift_right_logical(code, 4 * (source - group + HALF)) & 15
            at = piece * per_rep + column - source * blocks_group - first
            sums[at] += held[block, s].astype(F32)
        for c in range(columns):
            lanes = slice(c % per_rep * side, (c % per_rep + 1) * side)
            out_ref[c // per_rep, rows_of(block), lanes] = sums[c].astype(BF16)
        return carry

    lax.fori_loop(0, blocks, step, 0)


def dense_band(cols, vals, blocks_group, per_rep):
    blocks, count, side, _ = vals.shape
    columns = SECTIONS * per_rep
    shape = (SECTIONS, blocks * side, per_rep * side)

    def kernel(*refs):
        band_kernel(blocks_group, per_rep, *refs)

    return pl.pallas_call(
        kernel,
        in_specs=[pl.BlockSpec(memory_space=pltpu.SMEM), pl.BlockSpec(memory_space=pltpu.HBM)],
        out_specs=pl.BlockSpec(memory_space=pltpu.VMEM),
        out_shape=jax.ShapeDtypeStruct(shape, BF16),
        scratch_shapes=[
            pltpu.VMEM(vals.shape, BF16),
            pltpu.VMEM((columns, side, side), F32),
            pltpu.SemaphoreType.DMA((blocks,)),
        ],
        compiler_params=params(16),
        cost_estimate=cost(4),
        name="dense_band",
    )(pltpu.with_memory_space_constraint(cols, pltpu.HBM), pltpu.with_memory_space_constraint(vals, pltpu.HBM))


def aggregate_kernel(band_ref, near_ref, other_ref, far_ref, out_ref):
    reps, rows, hidden = out_ref.shape
    for q in range(reps):
        total = jnp.zeros((rows, hidden), F32)
        piece = 0
        for ref in (near_ref, other_ref, far_ref):
            for k in range(ref.shape[0] // rows):
                total = total + jnp.dot(
                    band_ref[piece, q * rows : (q + 1) * rows, :],
                    ref[k * rows : (k + 1) * rows, :],
                    preferred_element_type=F32,
                )
                piece += 1
        out_ref[q] = total.astype(BF16)


def partial_aggregate(band, near, other, far, reps):
    rows, hidden = band.shape[1] // reps, near.shape[1]
    return pl.pallas_call(
        aggregate_kernel,
        out_shape=jax.ShapeDtypeStruct((reps, rows, hidden), BF16),
        compiler_params=params(12),
        cost_estimate=cost(1.5),
        name="partial_aggregate",
    )(band, near, other, far)


def dense_kernel(parts_ref, weight_ref, cotangent_ref, out_ref, back_ref, local_ref):
    reps, rows, hidden = parts_ref.shape
    summed = parts_ref[0].astype(F32)
    for q in range(1, reps):
        summed = summed + parts_ref[q].astype(F32)
    aggregate = summed.astype(BF16)
    preact = jnp.dot(aggregate, weight_ref[...], preferred_element_type=F32)
    sigmoid_pre = 1.0 / (1.0 + jnp.exp(-preact))
    grad_pre = (
        cotangent_ref[...].astype(F32) * sigmoid_pre * (1.0 + preact * (1.0 - sigmoid_pre))
    ).astype(BF16)
    back_ref[...] = lax.dot_general(
        weight_ref[...], grad_pre, (((1,), (1,)), ((), ())), preferred_element_type=F32
    ).astype(BF16)
    local_ref[...] = lax.dot_general(
        aggregate, grad_pre, (((0,), (0,)), ((), ())), preferred_element_type=F32
    )
    out_ref[...] = (preact * sigmoid_pre).astype(BF16)


def dense_layer(parts, weight, cotangent):
    reps, rows, hidden = parts.shape
    return pl.pallas_call(
        dense_kernel,
        out_shape=(
            jax.ShapeDtypeStruct((rows, hidden), BF16),
            jax.ShapeDtypeStruct((hidden, rows), BF16),
            jax.ShapeDtypeStruct((hidden, hidden), F32),
        ),
        compiler_params=params(8),
        cost_estimate=cost(1.3),
        name="dense_layer",
    )(parts, weight, cotangent)


def gradient_kernel(reps, band_ref, *refs):
    near_ref, other_ref, far_ref, held, arrived = refs[reps:]
    hidden, rows = far_ref.shape
    rep = lax.axis_index("rep")

    def fetch(piece):
        return pltpu.make_async_copy(band_ref.at[piece], held.at[piece], arrived.at[piece])

    order = [*range(HALF, 2 * HALF + 1), *range(HALF)]
    for piece in order:
        fetch(piece).start()
    for piece in order:
        fetch(piece).wait()
        total = jnp.zeros((hidden, rows), F32)
        for k in range(reps):
            at = pl.multiple_of(lax.rem(rep + k, reps) * rows, rows)
            total = total + jnp.dot(
                refs[k][...], held[piece, pl.ds(at, rows), :], preferred_element_type=F32
            )
        if piece < HALF:
            near_ref[piece * hidden : (piece + 1) * hidden, :] = total
        elif piece < 2 * HALF:
            other_ref[(piece - HALF) * hidden : (piece - HALF + 1) * hidden, :] = total.astype(BF16)
        else:
            far_ref[...] = total.astype(BF16)


def window_gradient(band, back):
    reps = len(back)
    hidden, rows = back[0].shape

    def kernel(*refs):
        gradient_kernel(reps, *refs)

    return pl.pallas_call(
        kernel,
        in_specs=[pl.BlockSpec(memory_space=pltpu.HBM)] + [pl.BlockSpec(memory_space=pltpu.VMEM)] * reps,
        out_shape=(
            jax.ShapeDtypeStruct((HALF * hidden, rows), F32),
            jax.ShapeDtypeStruct((HALF * hidden, rows), BF16),
            jax.ShapeDtypeStruct((hidden, rows), BF16),
        ),
        scratch_shapes=[pltpu.VMEM(band.shape, BF16), pltpu.SemaphoreType.DMA((SECTIONS,))],
        compiler_params=params(12),
        cost_estimate=cost(GRADIENT_US),
        name="window_gradient",
    )(pltpu.with_memory_space_constraint(band, pltpu.HBM), *back)


def chip_sum_kernel(near_ref, swapped_ref, own_ref, before_ref, after_ref):
    rows = own_ref.shape[0]
    for k, ref in enumerate((own_ref, before_ref, after_ref)):
        at = slice(k * rows, (k + 1) * rows)
        ref[...] = (near_ref[at, :] + swapped_ref[at, :].astype(F32)).astype(ref.dtype)


def chip_sum(near, swapped):
    rows, hidden = near.shape[0] // HALF, near.shape[1]
    return pl.pallas_call(
        chip_sum_kernel,
        out_shape=tuple(jax.ShapeDtypeStruct((rows, hidden), t) for t in (F32, BF16, BF16)),
        compiler_params=params(8),
        cost_estimate=cost(CHIP_SUM_US),
        name="chip_sum",
    )(near, swapped)


def total_kernel(own_ref, after_ref, before_ref, far_ref, out_ref):
    total = own_ref[...]
    for ref in (after_ref, before_ref, far_ref):
        total = total + ref[...].astype(F32)
    out_ref[...] = total.T


def total_gradient(own, after, before, far):
    hidden, rows = own.shape
    return pl.pallas_call(
        total_kernel,
        out_shape=jax.ShapeDtypeStruct((rows, hidden), F32),
        compiler_params=params(8),
        cost_estimate=cost(0.6),
        name="total_gradient",
    )(own, after, before, far)


def spread_kernel(scale, terms_ref, out_ref):
    total = terms_ref[0].astype(F32)
    for k in range(1, terms_ref.shape[0]):
        total = total + terms_ref[k].astype(F32)
    if scale is not None:
        total = total * scale
    total = total.astype(out_ref.dtype)
    for k in range(out_ref.shape[0]):
        out_ref[k] = total


def sum_and_spread(terms, copies, dtype, scale=None):
    def kernel(*refs):
        spread_kernel(scale, *refs)

    return pl.pallas_call(
        kernel,
        out_shape=jax.ShapeDtypeStruct((copies,) + terms.shape[1:], dtype),
        compiler_params=params(8),
        cost_estimate=cost(0.4),
        name="sum_and_spread",
    )(terms)


def on_device(features, block_cols, block_vals, weight, cotangent):
    reps = lax.axis_size("rep")
    group_rows, hidden = features.shape
    side = block_vals.shape[-1]
    blocks_group = group_rows // side
    per_rep = blocks_group // reps
    rows = per_rep * side

    own = own_quarter(features, rows)
    before = chip_shift(own, 1)
    after = chip_shift(own, -1)
    far = far_shift(own)
    band = dense_band(block_cols, block_vals[:, 0], blocks_group, per_rep)
    before, after, far, band = lax.optimization_barrier((before, after, far, band))

    near = jnp.concatenate([own, before, after], axis=0)
    other = core_swap(near)
    parts = to_all(partial_aggregate(band, near, other, far, reps), "rep")

    output_rows, backward, local = dense_layer(parts, weight, cotangent)
    line = lax.axis_size("z")
    plane = lax.axis_size(PLANE)
    node_count = group_rows * lax.axis_size(ROW)
    back = [backward] + [rep_shift(backward, k) for k in range(1, reps)]
    terms = to_all(local.reshape(plane, -1, hidden), PLANE)

    spread = sum_and_spread(terms, line, F32)
    terms = to_all(spread, "z")
    band, _ = lax.optimization_barrier((band, spread))
    near_grad, other_grad, far_grad = window_gradient(band, back)
    swapped = core_swap(other_grad)
    from_far = far_shift(far_grad)
    own_grad, before_grad, after_grad = chip_sum(near_grad, swapped)
    from_after = chip_shift(before_grad, -1)
    terms, _ = lax.optimization_barrier((terms, before_grad))
    spread = sum_and_spread(terms, plane, BF16, node_count ** (-0.5))
    terms = to_all(spread, PLANE)
    after_grad, _ = lax.optimization_barrier((after_grad, spread))
    from_before = chip_shift(after_grad, 1)
    grad_features = total_gradient(own_grad, from_after, from_before, from_far)
    terms, from_far, from_after = lax.optimization_barrier((terms, from_far, from_after))
    grad_weight = terms.reshape(hidden, hidden).astype(F32)
    return output_rows, grad_weight, grad_features


def solution(mesh):
    devices = mesh.devices
    split = Mesh(devices.reshape(X_CHIPS, -1, CORES, devices.shape[1]), ROW + ("rep",))
    everywhere = ROW + ("rep",)
    return jax.shard_map(
        on_device,
        mesh=split,
        in_specs=(
            P(ROW, None),
            P(ROW, "rep", None),
            P(ROW, "rep", None, None, None),
            P(),
            P(everywhere, None),
        ),
        out_specs=(P(everywhere, None), P(), P(everywhere, None)),
        check_vma=False,
    )
```

```python
import jax
import jax.numpy as jnp
from jax import lax
from jax.experimental import pallas as pl
from jax.experimental.pallas import tpu as pltpu
from jax.sharding import Mesh
from jax.sharding import PartitionSpec as P

HALF = 3
SECTIONS = 2 * HALF + 1
CORES = 2
X_CHIPS = 4
ROW = ("x", "z", "core")
PLANE = ("x", "core", "rep")
BF16 = jnp.bfloat16
F32 = jnp.float32
PIECE_OF = ((6, 1, 4, 0, 3, 2, 5), (4, 1, 3, 0, 5, 2, 6))
PIECE_CODE = tuple(sum(p << (4 * d) for d, p in enumerate(row)) for row in PIECE_OF)


GRADIENT_US = 2.0
CHIP_SUM_US = 0.5


def cost(us):
    return pl.CostEstimate(flops=0, transcendentals=0, bytes_accessed=int(us * 3.6e6))


def params(mib):
    return pltpu.CompilerParams(vmem_limit_bytes=mib << 20)


def chip_shift(x, by):
    devices = lax.axis_size(ROW)
    by = by * CORES
    return lax.ppermute(x, ROW, [(i, i + by) for i in range(devices) if 0 <= i + by < devices])


def far_shift(x):
    devices = lax.axis_size(ROW)
    pairs = []
    for i in range(devices):
        to = i + HALF if i % CORES else i - HALF
        if 0 <= to < devices:
            pairs.append((i, to))
    return lax.ppermute(x, ROW, pairs)


def core_swap(x):
    return lax.ppermute(x, "core", [(0, 1), (1, 0)])


def rep_shift(x, by):
    devices = lax.axis_size("rep")
    return lax.ppermute(x, "rep", [(i, (i - by) % devices) for i in range(devices)])


def to_all(x, axes):
    return lax.all_to_all(x, axes, 0, 0, tiled=False)


def quarter_kernel(features_ref, out_ref, arrived):
    rows = out_ref.shape[0]
    at = pl.multiple_of(lax.axis_index("rep") * rows, rows)
    fetch = pltpu.make_async_copy(features_ref.at[pl.ds(at, rows), :], out_ref, arrived)
    fetch.start()
    fetch.wait()


def own_quarter(features, rows):
    return pl.pallas_call(
        quarter_kernel,
        in_specs=[pl.BlockSpec(memory_space=pltpu.HBM)],
        out_specs=pl.BlockSpec(memory_space=pltpu.VMEM),
        out_shape=jax.ShapeDtypeStruct((rows, features.shape[1]), features.dtype),
        scratch_shapes=[pltpu.SemaphoreType.DMA(())],
        compiler_params=params(4),
        cost_estimate=cost(0.5),
        name="own_quarter",
    )(pltpu.with_memory_space_constraint(features, pltpu.HBM))


def band_kernel(blocks_group, per_rep, cols_ref, vals_ref, out_ref, held, sums, arrived):
    blocks, slots, side = held.shape[:3]
    columns = sums.shape[0]
    group = lax.axis_index(ROW)
    first = lax.axis_index("rep") * per_rep
    code = jnp.where(lax.axis_index("core") == 0, PIECE_CODE[0], PIECE_CODE[1])

    def fetch(block):
        return pltpu.make_async_copy(vals_ref.at[block], held.at[block], arrived.at[block])

    def rows_of(block):
        return pl.ds(pl.multiple_of(block * side, side), side)

    for block in range(blocks):
        fetch(block).start()

    def step(block, carry):
        fetch(block).wait()
        sums[...] = jnp.zeros_like(sums)
        for s in range(slots):
            column = cols_ref[block, 0, s]
            source = lax.div(column, blocks_group)
            piece = lax.shift_right_logical(code, 4 * (source - group + HALF)) & 15
            at = piece * per_rep + column - source * blocks_group - first
            sums[at] += held[block, s].astype(F32)
        for c in range(columns):
            lanes = slice(c % per_rep * side, (c % per_rep + 1) * side)
            out_ref[c // per_rep, rows_of(block), lanes] = sums[c].astype(BF16)
        return carry

    lax.fori_loop(0, blocks, step, 0)


def dense_band(cols, vals, blocks_group, per_rep):
    blocks, count, side, _ = vals.shape
    columns = SECTIONS * per_rep
    shape = (SECTIONS, blocks * side, per_rep * side)

    def kernel(*refs):
        band_kernel(blocks_group, per_rep, *refs)

    return pl.pallas_call(
        kernel,
        in_specs=[pl.BlockSpec(memory_space=pltpu.SMEM), pl.BlockSpec(memory_space=pltpu.HBM)],
        out_specs=pl.BlockSpec(memory_space=pltpu.VMEM),
        out_shape=jax.ShapeDtypeStruct(shape, BF16),
        scratch_shapes=[
            pltpu.VMEM(vals.shape, BF16),
            pltpu.VMEM((columns, side, side), F32),
            pltpu.SemaphoreType.DMA((blocks,)),
        ],
        compiler_params=params(16),
        cost_estimate=cost(4),
        name="dense_band",
    )(pltpu.with_memory_space_constraint(cols, pltpu.HBM), pltpu.with_memory_space_constraint(vals, pltpu.HBM))


def aggregate_kernel(band_ref, near_ref, other_ref, far_ref, out_ref):
    reps, rows, hidden = out_ref.shape
    for q in range(reps):
        total = jnp.zeros((rows, hidden), F32)
        piece = 0
        for ref in (near_ref, other_ref, far_ref):
            for k in range(ref.shape[0] // rows):
                total = total + jnp.dot(
                    band_ref[piece, q * rows : (q + 1) * rows, :],
                    ref[k * rows : (k + 1) * rows, :],
                    preferred_element_type=F32,
                )
                piece += 1
        out_ref[q] = total.astype(BF16)


def partial_aggregate(band, near, other, far, reps):
    rows, hidden = band.shape[1] // reps, near.shape[1]
    return pl.pallas_call(
        aggregate_kernel,
        out_shape=jax.ShapeDtypeStruct((reps, rows, hidden), BF16),
        compiler_params=params(12),
        cost_estimate=cost(1.5),
        name="partial_aggregate",
    )(band, near, other, far)


def dense_kernel(parts_ref, weight_ref, cotangent_ref, out_ref, back_ref, local_ref):
    reps, rows, hidden = parts_ref.shape
    summed = parts_ref[0].astype(F32)
    for q in range(1, reps):
        summed = summed + parts_ref[q].astype(F32)
    aggregate = summed.astype(BF16)
    preact = jnp.dot(aggregate, weight_ref[...], preferred_element_type=F32)
    sigmoid_pre = 1.0 / (1.0 + jnp.exp(-preact))
    grad_pre = (
        cotangent_ref[...].astype(F32) * sigmoid_pre * (1.0 + preact * (1.0 - sigmoid_pre))
    ).astype(BF16)
    back_ref[...] = lax.dot_general(
        weight_ref[...], grad_pre, (((1,), (1,)), ((), ())), preferred_element_type=F32
    ).astype(BF16)
    local = lax.dot_general(
        aggregate, grad_pre, (((0,), (0,)), ((), ())), preferred_element_type=F32
    )
    piece = local_ref.shape[1]
    for k in range(local_ref.shape[0]):
        local_ref[k] = local[k * piece : (k + 1) * piece].astype(BF16)
    out_ref[...] = (preact * sigmoid_pre).astype(BF16)


def dense_layer(parts, weight, cotangent):
    reps, rows, hidden = parts.shape
    plane = X_CHIPS * CORES * reps
    return pl.pallas_call(
        dense_kernel,
        out_shape=(
            jax.ShapeDtypeStruct((rows, hidden), BF16),
            jax.ShapeDtypeStruct((hidden, rows), BF16),
            jax.ShapeDtypeStruct((plane, hidden // plane, hidden), BF16),
        ),
        compiler_params=params(8),
        cost_estimate=cost(1.3),
        name="dense_layer",
    )(parts, weight, cotangent)


def gradient_kernel(reps, band_ref, *refs):
    near_ref, other_ref, far_ref, held, arrived = refs[reps:]
    hidden, rows = far_ref.shape
    rep = lax.axis_index("rep")

    groups = (slice(HALF, SECTIONS), slice(0, HALF))

    def fetch(turn):
        at = groups[turn]
        return pltpu.make_async_copy(band_ref.at[at], held.at[at], arrived.at[turn])

    for turn in range(len(groups)):
        fetch(turn).start()
    for piece in (*range(HALF, SECTIONS), *range(HALF)):
        if piece in (HALF, 0):
            fetch(0 if piece else 1).wait()
        total = jnp.zeros((hidden, rows), F32)
        for k in range(reps):
            at = pl.multiple_of(lax.rem(rep + k, reps) * rows, rows)
            total = total + jnp.dot(
                refs[k][...], held[piece, pl.ds(at, rows), :], preferred_element_type=F32
            )
        if piece < HALF:
            near_ref[piece * hidden : (piece + 1) * hidden, :] = total
        elif piece < 2 * HALF:
            other_ref[(piece - HALF) * hidden : (piece - HALF + 1) * hidden, :] = total.astype(BF16)
        else:
            far_ref[...] = total.astype(BF16)


def window_gradient(band, back):
    reps = len(back)
    hidden, rows = back[0].shape

    def kernel(*refs):
        gradient_kernel(reps, *refs)

    return pl.pallas_call(
        kernel,
        in_specs=[pl.BlockSpec(memory_space=pltpu.HBM)] + [pl.BlockSpec(memory_space=pltpu.VMEM)] * reps,
        out_shape=(
            jax.ShapeDtypeStruct((HALF * hidden, rows), F32),
            jax.ShapeDtypeStruct((HALF * hidden, rows), BF16),
            jax.ShapeDtypeStruct((hidden, rows), BF16),
        ),
        scratch_shapes=[pltpu.VMEM(band.shape, BF16), pltpu.SemaphoreType.DMA((2,))],
        compiler_params=params(12),
        cost_estimate=cost(GRADIENT_US),
        name="window_gradient",
    )(pltpu.with_memory_space_constraint(band, pltpu.HBM), *back)


def chip_sum_kernel(near_ref, swapped_ref, own_ref, before_ref, after_ref):
    rows = own_ref.shape[0]
    for k, ref in enumerate((own_ref, before_ref, after_ref)):
        at = slice(k * rows, (k + 1) * rows)
        ref[...] = (near_ref[at, :] + swapped_ref[at, :].astype(F32)).astype(ref.dtype)


def chip_sum(near, swapped):
    rows, hidden = near.shape[0] // HALF, near.shape[1]
    return pl.pallas_call(
        chip_sum_kernel,
        out_shape=tuple(jax.ShapeDtypeStruct((rows, hidden), t) for t in (F32, BF16, BF16)),
        compiler_params=params(8),
        cost_estimate=cost(CHIP_SUM_US),
        name="chip_sum",
    )(near, swapped)


def total_kernel(own_ref, after_ref, before_ref, far_ref, out_ref):
    total = own_ref[...]
    for ref in (after_ref, before_ref, far_ref):
        total = total + ref[...].astype(F32)
    out_ref[...] = total.T


def total_gradient(own, after, before, far):
    hidden, rows = own.shape
    return pl.pallas_call(
        total_kernel,
        out_shape=jax.ShapeDtypeStruct((rows, hidden), F32),
        compiler_params=params(8),
        cost_estimate=cost(0.6),
        name="total_gradient",
    )(own, after, before, far)


def spread_kernel(scale, terms_ref, out_ref):
    total = terms_ref[0].astype(F32)
    for k in range(1, terms_ref.shape[0]):
        total = total + terms_ref[k].astype(F32)
    if scale is not None:
        total = total * scale
    total = total.astype(out_ref.dtype)
    for k in range(out_ref.shape[0]):
        out_ref[k] = total


def sum_and_spread(terms, copies, dtype, scale=None):
    def kernel(*refs):
        spread_kernel(scale, *refs)

    return pl.pallas_call(
        kernel,
        out_shape=jax.ShapeDtypeStruct((copies,) + terms.shape[1:], dtype),
        compiler_params=params(8),
        cost_estimate=cost(0.4),
        name="sum_and_spread",
    )(terms)


def on_device(features, block_cols, block_vals, weight, cotangent):
    reps = lax.axis_size("rep")
    group_rows, hidden = features.shape
    side = block_vals.shape[-1]
    blocks_group = group_rows // side
    per_rep = blocks_group // reps
    rows = per_rep * side

    own = own_quarter(features, rows)
    before = chip_shift(own, 1)
    after = chip_shift(own, -1)
    far = far_shift(own)
    band = dense_band(block_cols, block_vals[:, 0], blocks_group, per_rep)
    before, after, far, band = lax.optimization_barrier((before, after, far, band))

    near = jnp.concatenate([own, before, after], axis=0)
    other = core_swap(near)
    parts = to_all(partial_aggregate(band, near, other, far, reps), "rep")

    output_rows, backward, local = dense_layer(parts, weight, cotangent)
    line = lax.axis_size("z")
    plane = lax.axis_size(PLANE)
    node_count = group_rows * lax.axis_size(ROW)
    back = [backward] + [rep_shift(backward, k) for k in range(1, reps)]
    terms = to_all(local, PLANE)

    spread = sum_and_spread(terms, line, F32)
    terms = to_all(spread, "z")
    band, _ = lax.optimization_barrier((band, spread))
    near_grad, other_grad, far_grad = window_gradient(band, back)
    swapped = core_swap(other_grad)
    from_far = far_shift(far_grad)
    own_grad, before_grad, after_grad = chip_sum(near_grad, swapped)
    from_after = chip_shift(before_grad, -1)
    terms, _ = lax.optimization_barrier((terms, before_grad))
    spread = sum_and_spread(terms, plane, BF16, node_count ** (-0.5))
    terms = to_all(spread, PLANE)
    after_grad, _ = lax.optimization_barrier((after_grad, spread))
    from_before = chip_shift(after_grad, 1)
    grad_features = total_gradient(own_grad, from_after, from_before, from_far)
    terms, from_far, from_after = lax.optimization_barrier((terms, from_far, from_after))
    grad_weight = terms.reshape(hidden, hidden).astype(F32)
    return output_rows, grad_weight, grad_features


def solution(mesh):
    devices = mesh.devices
    split = Mesh(devices.reshape(X_CHIPS, -1, CORES, devices.shape[1]), ROW + ("rep",))
    everywhere = ROW + ("rep",)
    return jax.shard_map(
        on_device,
        mesh=split,
        in_specs=(
            P(ROW, None),
            P(ROW, "rep", None),
            P(ROW, "rep", None, None, None),
            P(),
            P(everywhere, None),
        ),
        out_specs=(P(everywhere, None), P(), P(everywhere, None)),
        check_vma=False,
    )
```

```python
import jax
import jax.numpy as jnp
from jax import lax
from jax.experimental import pallas as pl
from jax.experimental.pallas import tpu as pltpu
from jax.sharding import Mesh
from jax.sharding import PartitionSpec as P

HALF = 3
SECTIONS = 2 * HALF + 1
CORES = 2
X_CHIPS = 4
ROW = ("x", "z", "core")
PLANE = ("x", "core", "rep")
BF16 = jnp.bfloat16
F32 = jnp.float32
PIECE_OF = ((6, 1, 4, 0, 3, 2, 5), (4, 1, 3, 0, 5, 2, 6))
PIECE_CODE = tuple(sum(p << (4 * d) for d, p in enumerate(row)) for row in PIECE_OF)


GRADIENT_US = 2.0
CHIP_SUM_US = 0.5


def cost(us):
    return pl.CostEstimate(flops=0, transcendentals=0, bytes_accessed=int(us * 3.6e6))


def params(mib):
    return pltpu.CompilerParams(vmem_limit_bytes=mib << 20)


def chip_shift(x, by):
    devices = lax.axis_size(ROW)
    by = by * CORES
    return lax.ppermute(x, ROW, [(i, i + by) for i in range(devices) if 0 <= i + by < devices])


def far_shift(x):
    devices = lax.axis_size(ROW)
    pairs = []
    for i in range(devices):
        to = i + HALF if i % CORES else i - HALF
        if 0 <= to < devices:
            pairs.append((i, to))
    return lax.ppermute(x, ROW, pairs)


def core_swap(x):
    return lax.ppermute(x, "core", [(0, 1), (1, 0)])


def rep_shift(x, by):
    devices = lax.axis_size("rep")
    return lax.ppermute(x, "rep", [(i, (i - by) % devices) for i in range(devices)])


def to_all(x, axes):
    return lax.all_to_all(x, axes, 0, 0, tiled=False)


def quarter_kernel(features_ref, out_ref, arrived):
    rows = out_ref.shape[0]
    at = pl.multiple_of(lax.axis_index("rep") * rows, rows)
    fetch = pltpu.make_async_copy(features_ref.at[pl.ds(at, rows), :], out_ref, arrived)
    fetch.start()
    fetch.wait()


def own_quarter(features, rows):
    return pl.pallas_call(
        quarter_kernel,
        in_specs=[pl.BlockSpec(memory_space=pltpu.HBM)],
        out_specs=pl.BlockSpec(memory_space=pltpu.VMEM),
        out_shape=jax.ShapeDtypeStruct((rows, features.shape[1]), features.dtype),
        scratch_shapes=[pltpu.SemaphoreType.DMA(())],
        compiler_params=params(4),
        cost_estimate=cost(0.5),
        name="own_quarter",
    )(pltpu.with_memory_space_constraint(features, pltpu.HBM))


def band_kernel(blocks_group, per_rep, cols_ref, vals_ref, out_ref, held, sums, arrived):
    blocks, slots, side = held.shape[:3]
    columns = sums.shape[0]
    group = lax.axis_index(ROW)
    first = lax.axis_index("rep") * per_rep
    code = jnp.where(lax.axis_index("core") == 0, PIECE_CODE[0], PIECE_CODE[1])

    def fetch(block):
        return pltpu.make_async_copy(vals_ref.at[block], held.at[block], arrived.at[block])

    def rows_of(block):
        return pl.ds(pl.multiple_of(block * side, side), side)

    for block in range(blocks):
        fetch(block).start()

    def step(block, carry):
        fetch(block).wait()
        sums[...] = jnp.zeros_like(sums)
        for s in range(slots):
            column = cols_ref[block, 0, s]
            source = lax.div(column, blocks_group)
            piece = lax.shift_right_logical(code, 4 * (source - group + HALF)) & 15
            at = piece * per_rep + column - source * blocks_group - first
            sums[at] += held[block, s].astype(F32)
        for c in range(columns):
            lanes = slice(c % per_rep * side, (c % per_rep + 1) * side)
            out_ref[c // per_rep, rows_of(block), lanes] = sums[c].astype(BF16)
        return carry

    lax.fori_loop(0, blocks, step, 0)


def dense_band(cols, vals, blocks_group, per_rep):
    blocks, count, side, _ = vals.shape
    columns = SECTIONS * per_rep
    shape = (SECTIONS, blocks * side, per_rep * side)

    def kernel(*refs):
        band_kernel(blocks_group, per_rep, *refs)

    return pl.pallas_call(
        kernel,
        in_specs=[pl.BlockSpec(memory_space=pltpu.SMEM), pl.BlockSpec(memory_space=pltpu.HBM)],
        out_specs=pl.BlockSpec(memory_space=pltpu.VMEM),
        out_shape=jax.ShapeDtypeStruct(shape, BF16),
        scratch_shapes=[
            pltpu.VMEM(vals.shape, BF16),
            pltpu.VMEM((columns, side, side), F32),
            pltpu.SemaphoreType.DMA((blocks,)),
        ],
        compiler_params=params(16),
        cost_estimate=cost(4),
        name="dense_band",
    )(pltpu.with_memory_space_constraint(cols, pltpu.HBM), pltpu.with_memory_space_constraint(vals, pltpu.HBM))


def aggregate_kernel(band_ref, near_ref, other_ref, far_ref, out_ref):
    reps, rows, hidden = out_ref.shape
    for q in range(reps):
        total = jnp.zeros((rows, hidden), F32)
        piece = 0
        for ref in (near_ref, other_ref, far_ref):
            for k in range(ref.shape[0] // rows):
                total = total + jnp.dot(
                    band_ref[piece, q * rows : (q + 1) * rows, :],
                    ref[k * rows : (k + 1) * rows, :],
                    preferred_element_type=F32,
                )
                piece += 1
        out_ref[q] = total.astype(BF16)


def partial_aggregate(band, near, other, far, reps):
    rows, hidden = band.shape[1] // reps, near.shape[1]
    return pl.pallas_call(
        aggregate_kernel,
        out_shape=jax.ShapeDtypeStruct((reps, rows, hidden), BF16),
        compiler_params=params(12),
        cost_estimate=cost(1.5),
        name="partial_aggregate",
    )(band, near, other, far)


def dense_kernel(parts_ref, weight_ref, cotangent_ref, out_ref, back_ref, local_ref):
    reps, rows, hidden = parts_ref.shape
    summed = parts_ref[0].astype(F32)
    for q in range(1, reps):
        summed = summed + parts_ref[q].astype(F32)
    aggregate = summed.astype(BF16)
    preact = jnp.dot(aggregate, weight_ref[...], preferred_element_type=F32)
    sigmoid_pre = 1.0 / (1.0 + jnp.exp(-preact))
    grad_pre = (
        cotangent_ref[...].astype(F32) * sigmoid_pre * (1.0 + preact * (1.0 - sigmoid_pre))
    ).astype(BF16)
    back_ref[...] = lax.dot_general(
        weight_ref[...], grad_pre, (((1,), (1,)), ((), ())), preferred_element_type=F32
    ).astype(BF16)
    local = lax.dot_general(
        aggregate, grad_pre, (((0,), (0,)), ((), ())), preferred_element_type=F32
    )
    piece = local_ref.shape[1]
    for k in range(local_ref.shape[0]):
        local_ref[k] = local[k * piece : (k + 1) * piece].astype(BF16)
    out_ref[...] = (preact * sigmoid_pre).astype(BF16)


def dense_layer(parts, weight, cotangent):
    reps, rows, hidden = parts.shape
    plane = X_CHIPS * CORES * reps
    return pl.pallas_call(
        dense_kernel,
        out_shape=(
            jax.ShapeDtypeStruct((rows, hidden), BF16),
            jax.ShapeDtypeStruct((hidden, rows), BF16),
            jax.ShapeDtypeStruct((plane, hidden // plane, hidden), BF16),
        ),
        compiler_params=params(8),
        cost_estimate=cost(1.3),
        name="dense_layer",
    )(parts, weight, cotangent)


def gradient_kernel(steps, band_ref, *refs):
    reps = len(steps)
    near_ref, other_ref, far_ref, held, arrived = refs[reps:]
    hidden, rows = far_ref.shape
    rep = lax.axis_index("rep")

    groups = (slice(HALF, SECTIONS), slice(0, HALF))

    def fetch(turn):
        at = groups[turn]
        return pltpu.make_async_copy(band_ref.at[at], held.at[at], arrived.at[turn])

    for turn in range(len(groups)):
        fetch(turn).start()
    for piece in (*range(HALF, SECTIONS), *range(HALF)):
        if piece in (HALF, 0):
            fetch(0 if piece else 1).wait()
        total = jnp.zeros((hidden, rows), F32)
        for ref, k in zip(refs, steps):
            at = pl.multiple_of(lax.rem(rep + k, reps) * rows, rows)
            total = total + jnp.dot(
                ref[...], held[piece, pl.ds(at, rows), :], preferred_element_type=F32
            )
        if piece < HALF:
            near_ref[piece * hidden : (piece + 1) * hidden, :] = total
        elif piece < 2 * HALF:
            other_ref[(piece - HALF) * hidden : (piece - HALF + 1) * hidden, :] = total.astype(BF16)
        else:
            far_ref[...] = total.astype(BF16)


def window_gradient(band, back, order):
    reps = len(back)
    hidden, rows = back[0].shape

    def kernel(*refs):
        gradient_kernel(order, *refs)

    return pl.pallas_call(
        kernel,
        in_specs=[pl.BlockSpec(memory_space=pltpu.HBM)] + [pl.BlockSpec(memory_space=pltpu.VMEM)] * reps,
        out_shape=(
            jax.ShapeDtypeStruct((HALF * hidden, rows), F32),
            jax.ShapeDtypeStruct((HALF * hidden, rows), BF16),
            jax.ShapeDtypeStruct((hidden, rows), BF16),
        ),
        scratch_shapes=[pltpu.VMEM(band.shape, BF16), pltpu.SemaphoreType.DMA((2,))],
        compiler_params=params(12),
        cost_estimate=cost(GRADIENT_US),
        name="window_gradient",
    )(pltpu.with_memory_space_constraint(band, pltpu.HBM), *back)


def chip_sum_kernel(near_ref, swapped_ref, own_ref, before_ref, after_ref):
    rows = own_ref.shape[0]
    for k, ref in enumerate((own_ref, before_ref, after_ref)):
        at = slice(k * rows, (k + 1) * rows)
        ref[...] = (near_ref[at, :] + swapped_ref[at, :].astype(F32)).astype(ref.dtype)


def chip_sum(near, swapped):
    rows, hidden = near.shape[0] // HALF, near.shape[1]
    return pl.pallas_call(
        chip_sum_kernel,
        out_shape=tuple(jax.ShapeDtypeStruct((rows, hidden), t) for t in (F32, BF16, BF16)),
        compiler_params=params(8),
        cost_estimate=cost(CHIP_SUM_US),
        name="chip_sum",
    )(near, swapped)


def total_kernel(own_ref, after_ref, before_ref, far_ref, out_ref):
    total = own_ref[...]
    for ref in (after_ref, before_ref, far_ref):
        total = total + ref[...].astype(F32)
    out_ref[...] = total.T


def total_gradient(own, after, before, far):
    hidden, rows = own.shape
    return pl.pallas_call(
        total_kernel,
        out_shape=jax.ShapeDtypeStruct((rows, hidden), F32),
        compiler_params=params(8),
        cost_estimate=cost(0.6),
        name="total_gradient",
    )(own, after, before, far)


def spread_kernel(scale, terms_ref, out_ref):
    total = terms_ref[0].astype(F32)
    for k in range(1, terms_ref.shape[0]):
        total = total + terms_ref[k].astype(F32)
    if scale is not None:
        total = total * scale
    total = total.astype(out_ref.dtype)
    for k in range(out_ref.shape[0]):
        out_ref[k] = total


def sum_and_spread(terms, copies, dtype, scale=None):
    def kernel(*refs):
        spread_kernel(scale, *refs)

    return pl.pallas_call(
        kernel,
        out_shape=jax.ShapeDtypeStruct((copies,) + terms.shape[1:], dtype),
        compiler_params=params(8),
        cost_estimate=cost(0.4),
        name="sum_and_spread",
    )(terms)


def on_device(features, block_cols, block_vals, weight, cotangent):
    reps = lax.axis_size("rep")
    group_rows, hidden = features.shape
    side = block_vals.shape[-1]
    blocks_group = group_rows // side
    per_rep = blocks_group // reps
    rows = per_rep * side

    own = own_quarter(features, rows)
    before = chip_shift(own, 1)
    after = chip_shift(own, -1)
    far = far_shift(own)
    band = dense_band(block_cols, block_vals[:, 0], blocks_group, per_rep)
    before, after, far, band = lax.optimization_barrier((before, after, far, band))

    near = jnp.concatenate([own, before, after], axis=0)
    other = core_swap(near)
    parts = to_all(partial_aggregate(band, near, other, far, reps), "rep")

    output_rows, backward, local = dense_layer(parts, weight, cotangent)
    line = lax.axis_size("z")
    plane = lax.axis_size(PLANE)
    node_count = group_rows * lax.axis_size(ROW)
    order = [0, *range(2, reps, 2), *range(1, reps, 2)]
    back = [rep_shift(backward, k) if k else backward for k in order]
    terms = to_all(local, PLANE)

    spread = sum_and_spread(terms, line, F32)
    terms = to_all(spread, "z")
    band, _ = lax.optimization_barrier((band, spread))
    near_grad, other_grad, far_grad = window_gradient(band, back, order)
    swapped = core_swap(other_grad)
    from_far = far_shift(far_grad)
    own_grad, before_grad, after_grad = chip_sum(near_grad, swapped)
    from_after = chip_shift(before_grad, -1)
    terms, _ = lax.optimization_barrier((terms, before_grad))
    spread = sum_and_spread(terms, plane, BF16, node_count ** (-0.5))
    terms = to_all(spread, PLANE)
    after_grad, _ = lax.optimization_barrier((after_grad, spread))
    from_before = chip_shift(after_grad, 1)
    grad_features = total_gradient(own_grad, from_after, from_before, from_far)
    terms, from_far, from_after = lax.optimization_barrier((terms, from_far, from_after))
    grad_weight = terms.reshape(hidden, hidden).astype(F32)
    return output_rows, grad_weight, grad_features


def solution(mesh):
    devices = mesh.devices
    split = Mesh(devices.reshape(X_CHIPS, -1, CORES, devices.shape[1]), ROW + ("rep",))
    everywhere = ROW + ("rep",)
    return jax.shard_map(
        on_device,
        mesh=split,
        in_specs=(
            P(ROW, None),
            P(ROW, "rep", None),
            P(ROW, "rep", None, None, None),
            P(),
            P(everywhere, None),
        ),
        out_specs=(P(everywhere, None), P(), P(everywhere, None)),
        check_vma=False,
    )
```

```python
import jax
import jax.numpy as jnp
from jax import lax
from jax.experimental import pallas as pl
from jax.experimental.pallas import tpu as pltpu
from jax.sharding import Mesh
from jax.sharding import PartitionSpec as P

HALF = 3
SECTIONS = 2 * HALF + 1
CORES = 2
X_CHIPS = 4
ROW = ("x", "z", "core")
PLANE = ("x", "core", "rep")
BF16 = jnp.bfloat16
F32 = jnp.float32
PIECE_OF = ((6, 1, 4, 0, 3, 2, 5), (4, 1, 3, 0, 5, 2, 6))
TOGETHER = 2
PIECE_CODE = tuple(sum(p << (4 * d) for d, p in enumerate(row)) for row in PIECE_OF)


GRADIENT_US = 2.0
CHIP_SUM_US = 0.5


def cost(us):
    return pl.CostEstimate(flops=0, transcendentals=0, bytes_accessed=int(us * 3.6e6))


def params(mib):
    return pltpu.CompilerParams(vmem_limit_bytes=mib << 20)


def chip_shift(x, by):
    devices = lax.axis_size(ROW)
    by = by * CORES
    return lax.ppermute(x, ROW, [(i, i + by) for i in range(devices) if 0 <= i + by < devices])


def far_shift(x):
    devices = lax.axis_size(ROW)
    pairs = []
    for i in range(devices):
        to = i + HALF if i % CORES else i - HALF
        if 0 <= to < devices:
            pairs.append((i, to))
    return lax.ppermute(x, ROW, pairs)


def core_swap(x):
    return lax.ppermute(x, "core", [(0, 1), (1, 0)])


def rep_shift(x, by):
    devices = lax.axis_size("rep")
    return lax.ppermute(x, "rep", [(i, (i - by) % devices) for i in range(devices)])


def to_all(x, axes):
    return lax.all_to_all(x, axes, 0, 0, tiled=False)


def quarter_kernel(features_ref, out_ref, arrived):
    rows = out_ref.shape[0]
    at = pl.multiple_of(lax.axis_index("rep") * rows, rows)
    fetch = pltpu.make_async_copy(features_ref.at[pl.ds(at, rows), :], out_ref, arrived)
    fetch.start()
    fetch.wait()


def own_quarter(features, rows):
    return pl.pallas_call(
        quarter_kernel,
        in_specs=[pl.BlockSpec(memory_space=pltpu.HBM)],
        out_specs=pl.BlockSpec(memory_space=pltpu.VMEM),
        out_shape=jax.ShapeDtypeStruct((rows, features.shape[1]), features.dtype),
        scratch_shapes=[pltpu.SemaphoreType.DMA(())],
        compiler_params=params(4),
        cost_estimate=cost(0.5),
        name="own_quarter",
    )(pltpu.with_memory_space_constraint(features, pltpu.HBM))


def band_kernel(blocks_group, per_rep, cols_ref, vals_ref, out_ref, held, sums, arrived):
    blocks, slots, side = held.shape[:3]
    columns = sums.shape[0]
    group = lax.axis_index(ROW)
    first = lax.axis_index("rep") * per_rep
    code = jnp.where(lax.axis_index("core") == 0, PIECE_CODE[0], PIECE_CODE[1])

    def fetch(block):
        at = pl.ds(block * TOGETHER, TOGETHER)
        return pltpu.make_async_copy(vals_ref.at[at], held.at[at], arrived.at[block])

    def rows_of(block):
        return pl.ds(pl.multiple_of(block * side, side), side)

    for block in range(blocks // TOGETHER):
        fetch(block).start()

    def step(block, carry):
        @pl.when(lax.rem(block, TOGETHER) == 0)
        def _():
            fetch(lax.div(block, TOGETHER)).wait()

        sums[...] = jnp.zeros_like(sums)
        for s in range(slots):
            column = cols_ref[block, 0, s]
            source = lax.div(column, blocks_group)
            piece = lax.shift_right_logical(code, 4 * (source - group + HALF)) & 15
            at = piece * per_rep + column - source * blocks_group - first
            sums[at] += held[block, s].astype(F32)
        for c in range(columns):
            lanes = slice(c % per_rep * side, (c % per_rep + 1) * side)
            out_ref[c // per_rep, rows_of(block), lanes] = sums[c].astype(BF16)
        return carry

    lax.fori_loop(0, blocks, step, 0)


def dense_band(cols, vals, blocks_group, per_rep):
    blocks, count, side, _ = vals.shape
    columns = SECTIONS * per_rep
    shape = (SECTIONS, blocks * side, per_rep * side)

    def kernel(*refs):
        band_kernel(blocks_group, per_rep, *refs)

    return pl.pallas_call(
        kernel,
        in_specs=[pl.BlockSpec(memory_space=pltpu.SMEM), pl.BlockSpec(memory_space=pltpu.HBM)],
        out_specs=pl.BlockSpec(memory_space=pltpu.VMEM),
        out_shape=jax.ShapeDtypeStruct(shape, BF16),
        scratch_shapes=[
            pltpu.VMEM(vals.shape, BF16),
            pltpu.VMEM((columns, side, side), F32),
            pltpu.SemaphoreType.DMA((blocks // TOGETHER,)),
        ],
        compiler_params=params(16),
        cost_estimate=cost(4),
        name="dense_band",
    )(pltpu.with_memory_space_constraint(cols, pltpu.HBM), pltpu.with_memory_space_constraint(vals, pltpu.HBM))


def aggregate_kernel(band_ref, near_ref, other_ref, far_ref, out_ref):
    reps, rows, hidden = out_ref.shape
    for q in range(reps):
        total = jnp.zeros((rows, hidden), F32)
        piece = 0
        for ref in (near_ref, other_ref, far_ref):
            for k in range(ref.shape[0] // rows):
                total = total + jnp.dot(
                    band_ref[piece, q * rows : (q + 1) * rows, :],
                    ref[k * rows : (k + 1) * rows, :],
                    preferred_element_type=F32,
                )
                piece += 1
        out_ref[q] = total.astype(BF16)


def partial_aggregate(band, near, other, far, reps):
    rows, hidden = band.shape[1] // reps, near.shape[1]
    return pl.pallas_call(
        aggregate_kernel,
        out_shape=jax.ShapeDtypeStruct((reps, rows, hidden), BF16),
        compiler_params=params(12),
        cost_estimate=cost(1.5),
        name="partial_aggregate",
    )(band, near, other, far)


def dense_kernel(parts_ref, weight_ref, cotangent_ref, out_ref, back_ref, local_ref):
    reps, rows, hidden = parts_ref.shape
    summed = parts_ref[0].astype(F32)
    for q in range(1, reps):
        summed = summed + parts_ref[q].astype(F32)
    aggregate = summed.astype(BF16)
    preact = jnp.dot(aggregate, weight_ref[...], preferred_element_type=F32)
    sigmoid_pre = 1.0 / (1.0 + jnp.exp(-preact))
    grad_pre = (
        cotangent_ref[...].astype(F32) * sigmoid_pre * (1.0 + preact * (1.0 - sigmoid_pre))
    ).astype(BF16)
    back_ref[...] = lax.dot_general(
        weight_ref[...], grad_pre, (((1,), (1,)), ((), ())), preferred_element_type=F32
    ).astype(BF16)
    local = lax.dot_general(
        aggregate, grad_pre, (((0,), (0,)), ((), ())), preferred_element_type=F32
    )
    piece = local_ref.shape[1]
    for k in range(local_ref.shape[0]):
        local_ref[k] = local[k * piece : (k + 1) * piece].astype(BF16)
    out_ref[...] = (preact * sigmoid_pre).astype(BF16)


def dense_layer(parts, weight, cotangent):
    reps, rows, hidden = parts.shape
    plane = X_CHIPS * CORES * reps
    return pl.pallas_call(
        dense_kernel,
        out_shape=(
            jax.ShapeDtypeStruct((rows, hidden), BF16),
            jax.ShapeDtypeStruct((hidden, rows), BF16),
            jax.ShapeDtypeStruct((plane, hidden // plane, hidden), BF16),
        ),
        compiler_params=params(8),
        cost_estimate=cost(1.3),
        name="dense_layer",
    )(parts, weight, cotangent)


def gradient_kernel(reps, band_ref, *refs):
    near_ref, other_ref, far_ref, held, arrived = refs[reps:]
    hidden, rows = far_ref.shape
    rep = lax.axis_index("rep")

    groups = (slice(HALF, SECTIONS), slice(0, HALF))

    def fetch(turn):
        at = groups[turn]
        return pltpu.make_async_copy(band_ref.at[at], held.at[at], arrived.at[turn])

    for turn in range(len(groups)):
        fetch(turn).start()
    for piece in (*range(HALF, SECTIONS), *range(HALF)):
        if piece in (HALF, 0):
            fetch(0 if piece else 1).wait()
        total = jnp.zeros((hidden, rows), F32)
        for k in range(reps):
            at = pl.multiple_of(lax.rem(rep + k, reps) * rows, rows)
            total = total + jnp.dot(
                refs[k][...], held[piece, pl.ds(at, rows), :], preferred_element_type=F32
            )
        if piece < HALF:
            near_ref[piece * hidden : (piece + 1) * hidden, :] = total
        elif piece < 2 * HALF:
            other_ref[(piece - HALF) * hidden : (piece - HALF + 1) * hidden, :] = total.astype(BF16)
        else:
            far_ref[...] = total.astype(BF16)


def window_gradient(band, back):
    reps = len(back)
    hidden, rows = back[0].shape

    def kernel(*refs):
        gradient_kernel(reps, *refs)

    return pl.pallas_call(
        kernel,
        in_specs=[pl.BlockSpec(memory_space=pltpu.HBM)] + [pl.BlockSpec(memory_space=pltpu.VMEM)] * reps,
        out_shape=(
            jax.ShapeDtypeStruct((HALF * hidden, rows), F32),
            jax.ShapeDtypeStruct((HALF * hidden, rows), BF16),
            jax.ShapeDtypeStruct((hidden, rows), BF16),
        ),
        scratch_shapes=[pltpu.VMEM(band.shape, BF16), pltpu.SemaphoreType.DMA((2,))],
        compiler_params=params(12),
        cost_estimate=cost(GRADIENT_US),
        name="window_gradient",
    )(pltpu.with_memory_space_constraint(band, pltpu.HBM), *back)


def chip_sum_kernel(near_ref, swapped_ref, own_ref, before_ref, after_ref):
    rows = own_ref.shape[0]
    for k, ref in enumerate((own_ref, before_ref, after_ref)):
        at = slice(k * rows, (k + 1) * rows)
        ref[...] = (near_ref[at, :] + swapped_ref[at, :].astype(F32)).astype(ref.dtype)


def chip_sum(near, swapped):
    rows, hidden = near.shape[0] // HALF, near.shape[1]
    return pl.pallas_call(
        chip_sum_kernel,
        out_shape=tuple(jax.ShapeDtypeStruct((rows, hidden), t) for t in (F32, BF16, BF16)),
        compiler_params=params(8),
        cost_estimate=cost(CHIP_SUM_US),
        name="chip_sum",
    )(near, swapped)


def total_kernel(own_ref, after_ref, before_ref, far_ref, out_ref):
    total = own_ref[...]
    for ref in (after_ref, before_ref, far_ref):
        total = total + ref[...].astype(F32)
    out_ref[...] = total.T


def total_gradient(own, after, before, far):
    hidden, rows = own.shape
    return pl.pallas_call(
        total_kernel,
        out_shape=jax.ShapeDtypeStruct((rows, hidden), F32),
        compiler_params=params(8),
        cost_estimate=cost(0.6),
        name="total_gradient",
    )(own, after, before, far)


def spread_kernel(scale, terms_ref, out_ref):
    total = terms_ref[0].astype(F32)
    for k in range(1, terms_ref.shape[0]):
        total = total + terms_ref[k].astype(F32)
    if scale is not None:
        total = total * scale
    total = total.astype(out_ref.dtype)
    for k in range(out_ref.shape[0]):
        out_ref[k] = total


def sum_and_spread(terms, copies, dtype, scale=None):
    def kernel(*refs):
        spread_kernel(scale, *refs)

    return pl.pallas_call(
        kernel,
        out_shape=jax.ShapeDtypeStruct((copies,) + terms.shape[1:], dtype),
        compiler_params=params(8),
        cost_estimate=cost(0.4),
        name="sum_and_spread",
    )(terms)


def on_device(features, block_cols, block_vals, weight, cotangent):
    reps = lax.axis_size("rep")
    group_rows, hidden = features.shape
    side = block_vals.shape[-1]
    blocks_group = group_rows // side
    per_rep = blocks_group // reps
    rows = per_rep * side

    own = own_quarter(features, rows)
    before = chip_shift(own, 1)
    after = chip_shift(own, -1)
    far = far_shift(own)
    band = dense_band(block_cols, block_vals[:, 0], blocks_group, per_rep)
    before, after, far, band = lax.optimization_barrier((before, after, far, band))

    near = jnp.concatenate([own, before, after], axis=0)
    other = core_swap(near)
    parts = to_all(partial_aggregate(band, near, other, far, reps), "rep")

    output_rows, backward, local = dense_layer(parts, weight, cotangent)
    line = lax.axis_size("z")
    plane = lax.axis_size(PLANE)
    node_count = group_rows * lax.axis_size(ROW)
    back = [backward] + [rep_shift(backward, k) for k in range(1, reps)]
    terms = to_all(local, PLANE)

    spread = sum_and_spread(terms, line, F32)
    terms = to_all(spread, "z")
    band, _ = lax.optimization_barrier((band, spread))
    near_grad, other_grad, far_grad = window_gradient(band, back)
    swapped = core_swap(other_grad)
    from_far = far_shift(far_grad)
    own_grad, before_grad, after_grad = chip_sum(near_grad, swapped)
    from_after = chip_shift(before_grad, -1)
    terms, _ = lax.optimization_barrier((terms, before_grad))
    spread = sum_and_spread(terms, plane, BF16, node_count ** (-0.5))
    terms = to_all(spread, PLANE)
    after_grad, _ = lax.optimization_barrier((after_grad, spread))
    from_before = chip_shift(after_grad, 1)
    grad_features = total_gradient(own_grad, from_after, from_before, from_far)
    terms, from_far, from_after = lax.optimization_barrier((terms, from_far, from_after))
    grad_weight = terms.reshape(hidden, hidden).astype(F32)
    return output_rows, grad_weight, grad_features


def solution(mesh):
    devices = mesh.devices
    split = Mesh(devices.reshape(X_CHIPS, -1, CORES, devices.shape[1]), ROW + ("rep",))
    everywhere = ROW + ("rep",)
    return jax.shard_map(
        on_device,
        mesh=split,
        in_specs=(
            P(ROW, None),
            P(ROW, "rep", None),
            P(ROW, "rep", None, None, None),
            P(),
            P(everywhere, None),
        ),
        out_specs=(P(everywhere, None), P(), P(everywhere, None)),
        check_vma=False,
    )
```
